512 devices in a mesh: seq: 128 (over z, y, core), head: 4 (over x).
Axes of the slice: x: 4, y: 4, z: 16, core: 2. Of those that a mesh axis runs over, the one named last changes fastest.
Arguments:
- query: bfloat16 [6144, 1536], P('seq', 'head'), may hold values from -64 to 64
- new_kv: bfloat16 [2, 6144, 1536], P(None, 'seq', 'head'), may hold values from -6 to 6
- cache_kv: bfloat16 [2, 16384, 1536], P(None, 'seq', 'head'), may hold values from -6 to 6
- text_kv: bfloat16 [2, 512, 1536], P(None, None, 'head'), may hold values from -8 to 8
- active: int32 [6144], P('seq'), may hold values from 0 to 16383, as said below
- counts: int32 [128], P('seq'), may hold values from 0 to 48, as said below
- hidden: bfloat16 [6144, 3072], P('seq', 'head'), may hold values from -64 to 64
- w_out: bfloat16 [1536, 3072], P('head'), may hold values from -0.4375 to 0.4375
- mod_shift: float32 [3072], P('head'), may hold values from -3 to 3
- mod_scale: float32 [3072], P('head'), may hold values from -3 to 3
- w_final: float32 [3072, 64], P('head'), may hold values from -0.109375 to 0.109375
- latent: float32 [16384, 64], P('seq'), may hold values from -6 to 6
- cached_velocity: float32 [16384, 64], P('seq'), may hold values from -6 to 6
- step_size: float32 [1], replicated, may hold values from -0.6 to -0.1
Outputs:
- velocity: float32 [16384, 64], P('seq')
- latent_next: float32 [16384, 64], P('seq')
The draws below stay inside these ranges and needn't reach their ends.
Inputs may be any that keep to these rules, and one draw needn't show every extreme that they name: `active`: for shard k, the entries k * 48 to k * 48 + counts[k] - 1 are distinct image tokens of that shard (k * 128 to (k + 1) * 128 - 1); the later entries of the shard are tokens of the same shard and carry no meaning. The counts sum to exactly 24 times the number of shards; some shard has 48 and some shard has 0.
All inputs are finite; a program needn't handle non-finite values.
Results may differ from the reference program's by a relative error of at most 0.0035.
Values may be sent and summed in bfloat16 or wider, within the bound.
No kernel may reach another device: no remote copies, remote signals or barrier semaphores. Data moves between devices by JAX's collectives and lax.ppermute only.
A program may use at most 128 MiB of HBM per device.

```python
import math
import jax
import jax.numpy as jnp
from jax import lax

D = 3072
HEADS = 12
HD = 128
CH = 64
TEXT = 512
TOK_DEV = 128
ACT_DEV = 24
CAP = 48
TOKENS = 16384
SLOTS = 6144
HW = 1536
N_SEQ = 128


def active_plan(key):
    root_key = jax.random.fold_in(key, 11)
    shards = TOKENS // TOK_DEV
    ordering = jax.random.permutation(jax.random.fold_in(root_key, 1), shards)
    margin = CAP - ACT_DEV
    uplift = jax.random.randint(jax.random.fold_in(root_key, 2), (shards // 2,), 0, margin + 1)
    uplift = uplift.at[0].set(margin)
    counts = jnp.zeros((shards,), jnp.int32)
    counts = counts.at[ordering[0::2]].set(ACT_DEV + uplift)
    counts = counts.at[ordering[1::2]].set(ACT_DEV - uplift)
    pick_keys = jax.random.split(jax.random.fold_in(root_key, 3), shards)
    within = jax.vmap(lambda pick_key: jax.random.permutation(pick_key, TOK_DEV)[:CAP])(pick_keys)
    offsets = (jnp.arange(shards) * TOK_DEV)[:, None]
    return (counts.astype(jnp.int32), (within + offsets).reshape(-1).astype(jnp.int32))


def draw_active(key, part):
    return active_plan(key)[1]


def draw_counts(key, part):
    return active_plan(key)[0]


def attention_inputs(key):
    root_key = jax.random.fold_in(key, 23)
    queries = 2.5 * jax.random.truncated_normal(jax.random.fold_in(root_key, 1), -4.0, 4.0, (SLOTS, HW), jnp.float32)
    text_rows = jax.random.truncated_normal(jax.random.fold_in(root_key, 2), -4.0, 4.0, (2, TEXT, HW), jnp.float32)
    text_rows = text_rows.at[0].multiply(1.25)
    return (queries, text_rows)


def draw_query(key, part):
    return attention_inputs(key)[0].astype(jnp.bfloat16)


def draw_text_kv(key, part):
    return attention_inputs(key)[1].astype(jnp.bfloat16)


def draw_hidden(key, part):
    root_key = jax.random.fold_in(key, 31)
    col_log = jnp.arange(D, dtype=jnp.float32) / D * math.log(3.0) + jax.random.uniform(jax.random.fold_in(root_key, 1), (D,), jnp.float32, 0.0, math.log(10.0 / 3.0))
    row_log = jax.random.uniform(jax.random.fold_in(root_key, 2), (SLOTS, 1), jnp.float32, 0.0, math.log(10.0))
    noise = jax.random.truncated_normal(jax.random.fold_in(root_key, 3), -4.0, 4.0, (SLOTS, D), jnp.float32)
    return (0.1 * jnp.exp(row_log) * jnp.exp(col_log)[None, :] * noise).astype(jnp.bfloat16)


def level_of(stream_key, dims, cuts, least, high):
    loudness, own = 1.0, jax.random.fold_in(stream_key, 6)
    for dim, parts in cuts:
        steps = jnp.exp(jax.random.uniform(jax.random.fold_in(own, dim), (parts,), jnp.float32, least / len(cuts), high / len(cuts)))
        loudness = loudness * jnp.repeat(steps, dims[dim] // parts).reshape([-1 if axis == dim else 1 for axis in range(len(dims))])
    return loudness


def gaussian(stream_key, extent, scale, bound, cuts=(), kind=jnp.bfloat16):
    factor_of = level_of(stream_key, extent, cuts, -0.22, 0.18) if cuts else 1.0
    values = jax.random.normal(stream_key, extent, jnp.float32) * scale * factor_of
    return jnp.minimum(jnp.maximum(values, -bound), bound).astype(kind)


def setup_inputs(seed: int = 0) -> dict:
    seeds = jax.random.split(jax.random.key(seed), 15)
    return {
        "query": draw_query(jax.random.fold_in(seeds[14], 71), 0),
        "new_kv": gaussian(seeds[1], (2, SLOTS, HW), 1.0, 6.0, ((1, 128), (2, 4))),
        "cache_kv": gaussian(seeds[2], (2, TOKENS, HW), 1.0, 6.0, ((1, 128), (2, 4))),
        "text_kv": draw_text_kv(jax.random.fold_in(seeds[14], 71), 0),
        "active": draw_active(jax.random.fold_in(seeds[14], 71), 0),
        "counts": draw_counts(jax.random.fold_in(seeds[14], 71), 0),
        "hidden": draw_hidden(jax.random.fold_in(seeds[14], 71), 0),
        "w_out": gaussian(seeds[7], (HW, D), (HW // 8) ** -0.5, 0.4375, ((0, 4),)),
        "mod_shift": gaussian(seeds[8], (D,), 0.5, 3.0, ((0, 4),), jnp.float32),
        "mod_scale": gaussian(seeds[9], (D,), 0.5, 3.0, ((0, 4),), jnp.float32),
        "w_final": gaussian(seeds[10], (D, CH), D ** -0.5, 0.109375, ((0, 4),), jnp.float32),
        "latent": gaussian(seeds[11], (TOKENS, CH), 1.0, 6.0, ((0, 128),), jnp.float32),
        "cached_velocity": gaussian(seeds[12], (TOKENS, CH), 1.0, 6.0, ((0, 128),), jnp.float32),
        "step_size": jnp.clip(jax.random.uniform(seeds[13], (1,), jnp.float32, -0.6, -0.1), -0.6, -0.1),
    }


EPS = 1e-06

def reference(query, new_kv, cache_kv, text_kv, active, counts, hidden, w_out, mod_shift, mod_scale, w_final, latent, cached_velocity, step_size):
    slot_ids = jnp.arange(CAP * N_SEQ, dtype=jnp.int32)
    live_slots = slot_ids % CAP < counts[slot_ids // CAP]
    target = jnp.where(live_slots, active, TOKENS).astype(jnp.int32)
    image_kv = cache_kv.at[:, target].set(new_kv, mode='drop')
    all_keys = jnp.concatenate([image_kv[0], text_kv[0]], axis=0).astype(jnp.float32)
    all_values = jnp.concatenate([image_kv[1], text_kv[1]], axis=0).astype(jnp.float32)
    key_count = all_keys.shape[0]
    keys_split = all_keys.reshape(key_count, HEADS, HD)
    values_split = all_values.reshape(key_count, HEADS, HD)
    score_scale = HD ** (-0.5)

    def one_block(queries):
        split = queries.astype(jnp.float32).reshape(CAP, HEADS, HD)
        scores = jnp.einsum('qhd,khd->hqk', split, keys_split) * score_scale
        row_max = lax.optimization_barrier(jnp.max(scores, axis=2, keepdims=True))
        weights = jnp.exp(scores - row_max)
        weight_sum = lax.optimization_barrier(jnp.sum(weights, axis=2))
        rounded = lax.optimization_barrier(weights.astype(jnp.bfloat16)).astype(jnp.float32)
        numerator = jnp.einsum('hqk,khd->qhd', rounded, values_split)
        return (numerator / jnp.transpose(weight_sum)[:, :, None]).reshape(CAP, HW).astype(jnp.bfloat16)
    attended = lax.map(one_block, query.reshape(N_SEQ, CAP, HW)).reshape(CAP * N_SEQ, HW)
    projected = jnp.dot(attended, w_out, preferred_element_type=jnp.float32)
    residual_sum = hidden.astype(jnp.float32) + projected
    row_mean = lax.optimization_barrier(jnp.mean(residual_sum, axis=1, keepdims=True))
    row_var = lax.optimization_barrier(jnp.mean(jnp.square(residual_sum - row_mean), axis=1, keepdims=True))
    normed = (residual_sum - row_mean) / jnp.sqrt(row_var + EPS) * (1.0 + mod_scale) + mod_shift
    fresh = jnp.dot(normed, w_final, precision=lax.Precision.HIGHEST)
    velocity = cached_velocity.at[target].set(fresh, mode='drop')
    latent_next = latent + step_size[0] * velocity
    return (velocity, latent_next)
```

```python
import functools

import jax
import jax.numpy as jnp
from jax import lax
from jax.experimental import pallas as pl
from jax.experimental.pallas import tpu as pltpu
from jax.sharding import PartitionSpec as P

D = 3072
HD = 128
EPS = 1e-06
LOG2E = 1.4426950408889634
SCALE = HD ** (-0.5)
PLANE = 8
STAT = 8


f32 = jnp.float32
bf16 = jnp.bfloat16
VM = pl.BlockSpec(memory_space=pltpu.VMEM)
SM = pl.BlockSpec(memory_space=pltpu.SMEM)


def one_hot(pos_ref, info_ref, rows, cols):
    local = pos_ref[...] - info_ref[0]
    slot = lax.broadcasted_iota(jnp.int32, (1, cols), 1)
    local = jnp.where(slot < info_ref[1], local, -1)
    return lax.broadcasted_iota(jnp.int32, (rows, cols), 0) == local


def fill_kernel(info_ref, pos_ref, new_ref, cache_ref, out_ref):
    rows, cols = cache_ref.shape[1], new_ref.shape[1]
    matched = one_hot(pos_ref, info_ref, rows, cols)
    pick = matched.astype(f32)
    keep = jnp.max(pick, axis=1, keepdims=True) < 0.5
    pick = pick.astype(bf16)
    for s in range(2):
        placed = jnp.dot(pick, new_ref[s], preferred_element_type=f32)
        merged = jnp.where(keep, cache_ref[s].astype(f32), placed).astype(bf16)
        for y in range(out_ref.shape[0]):
            out_ref[y, s] = merged


def fill(info, pos, new_kv, cache_kv, copies):
    return pl.pallas_call(
        fill_kernel,
        out_shape=jax.ShapeDtypeStruct((copies,) + cache_kv.shape, bf16),
        in_specs=[SM, VM, VM, VM],
        out_specs=VM,
    )(info, pos, new_kv, cache_kv)


def attend_kernel(part_ref, q_ref, a_ref, b_ref, t_ref, out_ref, *, chunk):
    del part_ref
    slots = out_ref.shape[1] - STAT
    keys, values = [], []
    for ref in (a_ref, b_ref):
        n = ref.shape[0] * ref.shape[2]
        keys.append(ref[:, 0].reshape(n, HD))
        values.append(ref[:, 1].reshape(n, HD))
    keys.append(t_ref[0])
    values.append(t_ref[1])
    lane = lax.broadcasted_iota(jnp.int32, (slots, HD), 1)
    eye = lax.broadcasted_iota(jnp.int32, (slots, HD), 0) == lane
    row = lax.broadcasted_iota(jnp.int32, (STAT, HD), 0)
    for start in range(0, q_ref.shape[0], chunk):
        q = q_ref[pl.ds(start, chunk), :]
        scores = [
            lax.dot_general(q, k, (((1,), (1,)), ((), ())), preferred_element_type=f32)
            for k in keys
        ]
        top = functools.reduce(
            jnp.maximum, [jnp.max(s, axis=1, keepdims=True) for s in scores]
        )
        weights = [jnp.exp2((s - top) * (SCALE * LOG2E)) for s in scores]
        total = sum(jnp.sum(w, axis=1, keepdims=True) for w in weights)
        mixed = sum(
            jnp.dot(w.astype(bf16), v, preferred_element_type=f32)
            for w, v in zip(weights, values)
        )
        mixed = mixed / total
        spread = top * SCALE + jnp.log(total)
        for i in range(chunk // slots):
            d = start // slots + i
            out_ref[d, 0:slots, :] = mixed[i * slots : (i + 1) * slots].astype(bf16)
            column = spread[i * slots : (i + 1) * slots]
            line = jnp.sum(jnp.where(eye, column, 0.0), axis=0, keepdims=True)
            first = line.astype(bf16).astype(f32)
            second = (line - first).astype(bf16).astype(f32)
            third = line - first - second
            pieces = jnp.where(row == 0, first, jnp.where(row == 1, second, third))
            out_ref[d, slots : slots + STAT, :] = pieces.astype(bf16)


def attend(part, parts, queries, near, far, text_kv, slots, chunk):
    rows, width = queries.shape
    text_rows = text_kv.shape[1] // parts
    kv_spec = pl.BlockSpec(near.shape[:3] + (HD,), lambda h, part: (0, 0, 0, h))
    return pl.pallas_call(
        functools.partial(attend_kernel, chunk=chunk),
        out_shape=jax.ShapeDtypeStruct((parts, slots + STAT, width), bf16),
        grid_spec=pltpu.PrefetchScalarGridSpec(
            num_scalar_prefetch=1,
            grid=(width // HD,),
            in_specs=[
                pl.BlockSpec((rows, HD), lambda h, part: (0, h)),
                kv_spec,
                kv_spec,
                pl.BlockSpec((2, text_rows, HD), lambda h, part: (0, part[0], h)),
            ],
            out_specs=pl.BlockSpec((parts, slots + STAT, HD), lambda h, part: (0, 0, h)),
        ),
    )(part, queries, near, far, text_kv)


def merge_kernel(got_ref, w_ref, out_ref):
    parts, rows, width = got_ref.shape
    slots = rows - STAT
    heads = []
    for h in range(width // HD):
        cols = slice(h * HD, (h + 1) * HD)
        stat = got_ref[:, slots:rows, cols].astype(f32)
        spread = stat[:, 0] + stat[:, 1] + stat[:, 2]
        share = jnp.exp(spread - jnp.max(spread, axis=0, keepdims=True))
        share = share / jnp.sum(share, axis=0, keepdims=True)
        share = jnp.concatenate([share, jnp.zeros((HD - parts, HD), f32)], axis=0).T
        total = jnp.zeros((slots, HD), f32)
        for s in range(parts):
            total += got_ref[s, 0:slots, cols].astype(f32) * share[0:slots, s : s + 1]
        heads.append(total.astype(bf16))
    attended = jnp.concatenate(heads, axis=1)
    piece = out_ref.shape[2]
    for k in range(out_ref.shape[0]):
        out_ref[k] = jnp.dot(
            attended, w_ref[:, k * piece : (k + 1) * piece], preferred_element_type=f32
        ).astype(bf16)


def merge(got, w_out, groups):
    return pl.pallas_call(
        merge_kernel,
        out_shape=jax.ShapeDtypeStruct(
            (groups, got.shape[1] - STAT, w_out.shape[1] // groups), bf16
        ),
        in_specs=[VM, VM],
        out_specs=VM,
    )(got, w_out)


def norm_kernel(got_ref, hidden_ref, scale_ref, shift_ref, w_ref, out_ref):
    slots, width = hidden_ref.shape
    summed = hidden_ref[...].astype(f32)
    for k in range(got_ref.shape[0]):
        summed += got_ref[k].astype(f32)
    mean = jnp.sum(summed, axis=1, keepdims=True) * (1.0 / width)
    centred = summed - mean
    squares = jnp.sum(centred * centred, axis=1, keepdims=True)
    lifted = 1.0 + scale_ref[...]
    tail = lax.broadcasted_iota(jnp.int32, (STAT, width), 0)
    tail = jnp.where(tail == 0, lifted, jnp.where(tail == 1, shift_ref[...], 0.0))
    rows = jnp.concatenate([centred * lifted, tail], axis=0)
    mapped = jnp.dot(
        rows, w_ref[...], precision=lax.Precision.HIGHEST, preferred_element_type=f32
    )
    lane = lax.broadcasted_iota(jnp.int32, (slots, 64), 1)
    stat = jnp.where(lane == 0, mean, jnp.where(lane == 1, squares, 0.0))
    stat = jnp.concatenate([stat, jnp.zeros((STAT, 64), f32)], axis=0)
    block = jnp.concatenate([mapped, stat], axis=1)
    for k in range(out_ref.shape[0]):
        out_ref[k] = block


def norm(got, hidden, scale, shift, w_final):
    return pl.pallas_call(
        norm_kernel,
        out_shape=jax.ShapeDtypeStruct(
            (got.shape[0], hidden.shape[0] + STAT, 2 * w_final.shape[1]), f32
        ),
        in_specs=[VM] * 5,
        out_specs=VM,
    )(got, hidden, scale, shift, w_final)


def finish_kernel(
    info_ref, step_ref, pos_ref, got_ref, latent_ref, old_ref, velocity_ref, next_ref
):
    groups, rows, _ = got_ref.shape
    slots = rows - STAT
    ch = latent_ref.shape[1]
    blocks = [got_ref[k] for k in range(groups)]
    means = [b[0:slots, ch : ch + 1] for b in blocks]
    mean = sum(means) * (1.0 / groups)
    width = D // groups
    var = sum(b[0:slots, ch + 1 : ch + 2] for b in blocks)
    var = (var + width * sum((m - mean) * (m - mean) for m in means)) * (1.0 / D)
    mapped = sum(
        b[0:slots, 0:ch] + (m - mean) * b[slots : slots + 1, 0:ch]
        for b, m in zip(blocks, means)
    )
    base = sum(b[slots + 1 : slots + 2, 0:ch] for b in blocks)
    fresh = mapped * lax.rsqrt(var + EPS) + base
    tokens = latent_ref.shape[0]
    pick = one_hot(pos_ref, info_ref, tokens, slots).astype(f32)
    keep = jnp.max(pick, axis=1, keepdims=True) < 0.5
    chosen = jnp.dot(
        pick, fresh, precision=lax.Precision.HIGHEST, preferred_element_type=f32
    )
    velocity = jnp.where(keep, old_ref[...], chosen)
    velocity_ref[...] = velocity
    next_ref[...] = latent_ref[...] + step_ref[0] * velocity


def finish(info, step_size, pos, got, latent, cached_velocity):
    return pl.pallas_call(
        finish_kernel,
        out_shape=(
            jax.ShapeDtypeStruct(latent.shape, f32),
            jax.ShapeDtypeStruct(latent.shape, f32),
        ),
        in_specs=[SM, SM, VM, VM, VM, VM],
        out_specs=(VM, VM),
    )(info, step_size, pos, got, latent, cached_velocity)


def on_device(
    query,
    new_kv,
    cache_kv,
    text_kv,
    active,
    counts,
    hidden,
    w_out,
    mod_shift,
    mod_scale,
    w_final,
    latent,
    cached_velocity,
    step_size,
):
    shards = lax.axis_size("seq")
    groups = lax.axis_size("head")
    planes = shards // PLANE
    own = lax.axis_index("seq")
    slots = query.shape[0]
    tokens = cache_kv.shape[1]
    along_y = [
        [z * PLANE + y * 2 + c for y in range(PLANE // 2)]
        for z in range(planes)
        for c in range(2)
    ]
    along_z = [[z * PLANE + r for z in range(planes)] for r in range(PLANE)]
    partner = [(i, i ^ 1) for i in range(shards)]

    info = jnp.stack([own * tokens, counts[0]]).astype(jnp.int32)
    pos = active.reshape(1, slots)
    filled = fill(info, pos, new_kv, cache_kv, PLANE // 2)
    near = lax.all_to_all(
        filled, "seq", 0, 0, axis_index_groups=along_y, tiled=True
    )
    gathered = lax.all_gather(
        query, "seq", axis=0, axis_index_groups=along_z, tiled=True
    )
    far = lax.ppermute(near, "seq", partner)
    part = (own // PLANE).reshape(1).astype(jnp.int32)
    partial = attend(part, planes, gathered, near, far, text_kv, slots, 192)
    returned = lax.all_to_all(
        partial, "seq", 0, 0, axis_index_groups=along_z, tiled=True
    )
    terms = merge(returned, w_out, groups)
    terms = lax.all_to_all(terms, "head", 0, 0, tiled=True)
    stats = norm(
        terms, hidden, mod_scale.reshape(1, -1), mod_shift.reshape(1, -1), w_final
    )
    stats = lax.all_to_all(stats, "head", 0, 0, tiled=True)
    return finish(info, step_size, pos, stats, latent, cached_velocity)


def solution(mesh):
    in_specs = (
        P("seq", "head"),
        P(None, "seq", "head"),
        P(None, "seq", "head"),
        P(None, None, "head"),
        P("seq"),
        P("seq"),
        P("seq", "head"),
        P("head", None),
        P("head"),
        P("head"),
        P("head", None),
        P("seq", None),
        P("seq", None),
        P(),
    )
    out_specs = (P("seq", None), P("seq", None))
    return jax.shard_map(
        on_device, mesh=mesh, in_specs=in_specs, out_specs=out_specs, check_vma=False
    )
```

```python
import functools

import jax
import jax.numpy as jnp
from jax import lax
from jax.experimental import pallas as pl
from jax.experimental.pallas import tpu as pltpu
from jax.sharding import PartitionSpec as P


D = 3072
HD = 128
EPS = 1e-06
LOG2E = 1.4426950408889634
SCALE = HD ** (-0.5)
SEQ = ("zb", "za", "y", "core")
STAT = 8


f32 = jnp.float32
bf16 = jnp.bfloat16
VM = pl.BlockSpec(memory_space=pltpu.VMEM)
SM = pl.BlockSpec(memory_space=pltpu.SMEM)


def one_hot(pos_ref, info_ref, rows, cols):
    local = pos_ref[...] - info_ref[0]
    slot = lax.broadcasted_iota(jnp.int32, (1, cols), 1)
    local = jnp.where(slot < info_ref[1], local, -1)
    return lax.broadcasted_iota(jnp.int32, (rows, cols), 0) == local


def fill_kernel(info_ref, pos_ref, new_ref, cache_ref, out_ref):
    rows, cols = cache_ref.shape[1], new_ref.shape[1]
    matched = one_hot(pos_ref, info_ref, rows, cols)
    pick = matched.astype(f32)
    keep = jnp.max(pick, axis=1, keepdims=True) < 0.5
    pick = pick.astype(bf16)
    for s in range(2):
        placed = jnp.dot(pick, new_ref[s], preferred_element_type=f32)
        merged = jnp.where(keep, cache_ref[s].astype(f32), placed).astype(bf16)
        for y in range(out_ref.shape[0]):
            out_ref[y, s] = merged


def fill(info, pos, new_kv, cache_kv, copies):
    return pl.pallas_call(
        fill_kernel,
        out_shape=jax.ShapeDtypeStruct((copies,) + cache_kv.shape, bf16),
        in_specs=[SM, VM, VM, VM],
        out_specs=VM,
    )(info, pos, new_kv, cache_kv)


def attend_kernel(part_ref, q_ref, a_ref, b_ref, t_ref, out_ref, *, chunk):
    del part_ref
    slots = out_ref.shape[1] - STAT
    keys, values = [], []
    for ref in (a_ref, b_ref):
        n = ref.shape[0] * ref.shape[2]
        keys.append(ref[:, 0].reshape(n, HD))
        values.append(ref[:, 1].reshape(n, HD))
    keys.append(t_ref[0])
    values.append(t_ref[1])
    lane = lax.broadcasted_iota(jnp.int32, (slots, HD), 1)
    eye = lax.broadcasted_iota(jnp.int32, (slots, HD), 0) == lane
    row = lax.broadcasted_iota(jnp.int32, (STAT, HD), 0)
    for start in range(0, q_ref.shape[0], chunk):
        q = q_ref[pl.ds(start, chunk), :]
        scores = [
            lax.dot_general(q, k, (((1,), (1,)), ((), ())), preferred_element_type=f32)
            for k in keys
        ]
        top = functools.reduce(
            jnp.maximum, [jnp.max(s, axis=1, keepdims=True) for s in scores]
        )
        weights = [jnp.exp2((s - top) * (SCALE * LOG2E)) for s in scores]
        total = sum(jnp.sum(w, axis=1, keepdims=True) for w in weights)
        mixed = sum(
            jnp.dot(w.astype(bf16), v, preferred_element_type=f32)
            for w, v in zip(weights, values)
        )
        mixed = mixed / total
        spread = top * SCALE + jnp.log(total)
        for i in range(chunk // slots):
            d = start // slots + i
            out_ref[d, 0:slots, :] = mixed[i * slots : (i + 1) * slots].astype(bf16)
            column = spread[i * slots : (i + 1) * slots]
            line = jnp.sum(jnp.where(eye, column, 0.0), axis=0, keepdims=True)
            first = line.astype(bf16).astype(f32)
            second = (line - first).astype(bf16).astype(f32)
            third = line - first - second
            pieces = jnp.where(row == 0, first, jnp.where(row == 1, second, third))
            out_ref[d, slots : slots + STAT, :] = pieces.astype(bf16)


def attend(part, parts, queries, near, far, text_kv, slots, chunk):
    rows, width = queries.shape
    text_rows = text_kv.shape[1] // parts
    kv_spec = pl.BlockSpec(near.shape[:3] + (HD,), lambda h, part: (0, 0, 0, h))
    return pl.pallas_call(
        functools.partial(attend_kernel, chunk=chunk),
        out_shape=jax.ShapeDtypeStruct((parts, slots + STAT, width), bf16),
        grid_spec=pltpu.PrefetchScalarGridSpec(
            num_scalar_prefetch=1,
            grid=(width // HD,),
            in_specs=[
                pl.BlockSpec((rows, HD), lambda h, part: (0, h)),
                kv_spec,
                kv_spec,
                pl.BlockSpec((2, text_rows, HD), lambda h, part: (0, part[0], h)),
            ],
            out_specs=pl.BlockSpec((parts, slots + STAT, HD), lambda h, part: (0, 0, h)),
        ),
    )(part, queries, near, far, text_kv)


def merge_kernel(got_ref, w_ref, out_ref):
    parts, rows, width = got_ref.shape
    slots = rows - STAT
    heads = []
    for h in range(width // HD):
        cols = slice(h * HD, (h + 1) * HD)
        stat = got_ref[:, slots:rows, cols].astype(f32)
        spread = stat[:, 0] + stat[:, 1] + stat[:, 2]
        share = jnp.exp(spread - jnp.max(spread, axis=0, keepdims=True))
        share = share / jnp.sum(share, axis=0, keepdims=True)
        share = jnp.concatenate([share, jnp.zeros((HD - parts, HD), f32)], axis=0).T
        total = jnp.zeros((slots, HD), f32)
        for s in range(parts):
            total += got_ref[s, 0:slots, cols].astype(f32) * share[0:slots, s : s + 1]
        heads.append(total.astype(bf16))
    attended = jnp.concatenate(heads, axis=1)
    piece = out_ref.shape[2]
    for k in range(out_ref.shape[0]):
        out_ref[k] = jnp.dot(
            attended, w_ref[:, k * piece : (k + 1) * piece], preferred_element_type=f32
        ).astype(bf16)


def merge(got, w_out, groups):
    return pl.pallas_call(
        merge_kernel,
        out_shape=jax.ShapeDtypeStruct(
            (groups, got.shape[1] - STAT, w_out.shape[1] // groups), bf16
        ),
        in_specs=[VM, VM],
        out_specs=VM,
    )(got, w_out)


def norm_kernel(got_ref, hidden_ref, scale_ref, shift_ref, w_ref, out_ref):
    slots, width = hidden_ref.shape
    summed = hidden_ref[...].astype(f32)
    for k in range(got_ref.shape[0]):
        summed += got_ref[k].astype(f32)
    mean = jnp.sum(summed, axis=1, keepdims=True) * (1.0 / width)
    centred = summed - mean
    squares = jnp.sum(centred * centred, axis=1, keepdims=True)
    lifted = 1.0 + scale_ref[...]
    tail = lax.broadcasted_iota(jnp.int32, (STAT, width), 0)
    tail = jnp.where(tail == 0, lifted, jnp.where(tail == 1, shift_ref[...], 0.0))
    rows = jnp.concatenate([centred * lifted, tail], axis=0)
    mapped = lax.dot_general(
        rows,
        w_ref[...],
        (((1,), (1,)), ((), ())),
        precision=lax.Precision.HIGHEST,
        preferred_element_type=f32,
    )
    lane = lax.broadcasted_iota(jnp.int32, (slots, 64), 1)
    stat = jnp.where(lane == 0, mean, jnp.where(lane == 1, squares, 0.0))
    stat = jnp.concatenate([stat, jnp.zeros((STAT, 64), f32)], axis=0)
    block = jnp.concatenate([mapped, stat], axis=1)
    for k in range(out_ref.shape[0]):
        out_ref[k] = block


def norm(got, hidden, scale, shift, w_final):
    return pl.pallas_call(
        norm_kernel,
        out_shape=jax.ShapeDtypeStruct(
            (got.shape[0], hidden.shape[0] + STAT, 2 * w_final.shape[1]), f32
        ),
        in_specs=[VM] * 5,
        out_specs=VM,
    )(got, hidden, scale, shift, w_final.T)


def finish_kernel(
    info_ref, step_ref, pos_ref, got_ref, latent_ref, old_ref, velocity_ref, next_ref
):
    groups, rows, _ = got_ref.shape
    slots = rows - STAT
    ch = latent_ref.shape[0]
    blocks = [got_ref[k] for k in range(groups)]
    means = [b[0:slots, ch : ch + 1] for b in blocks]
    mean = sum(means) * (1.0 / groups)
    width = D // groups
    var = sum(b[0:slots, ch + 1 : ch + 2] for b in blocks)
    var = (var + width * sum((m - mean) * (m - mean) for m in means)) * (1.0 / D)
    mapped = sum(
        b[0:slots, 0:ch] + (m - mean) * b[slots : slots + 1, 0:ch]
        for b, m in zip(blocks, means)
    )
    base = sum(b[slots + 1 : slots + 2, 0:ch] for b in blocks)
    fresh = mapped * lax.rsqrt(var + EPS) + base
    tokens = latent_ref.shape[1]
    pick = one_hot(pos_ref, info_ref, tokens, slots).astype(f32)
    keep = lax.dot_general(
        jnp.ones((8, slots), f32),
        pick,
        (((1,), (1,)), ((), ())),
        preferred_element_type=f32,
    )[0:1]
    chosen = lax.dot_general(
        fresh,
        pick,
        (((0,), (1,)), ((), ())),
        precision=lax.Precision.HIGHEST,
        preferred_element_type=f32,
    )
    velocity = jnp.where(keep < 0.5, old_ref[...], chosen)
    velocity_ref[...] = velocity
    next_ref[...] = latent_ref[...] + step_ref[0] * velocity


def finish(info, step_size, pos, got, latent, cached_velocity):
    velocity, following = pl.pallas_call(
        finish_kernel,
        out_shape=(
            jax.ShapeDtypeStruct(latent.shape[::-1], f32),
            jax.ShapeDtypeStruct(latent.shape[::-1], f32),
        ),
        in_specs=[SM, SM, VM, VM, VM, VM],
        out_specs=(VM, VM),
    )(info, step_size, pos, got, latent.T, cached_velocity.T)
    return velocity.T, following.T


def on_device(
    query,
    new_kv,
    cache_kv,
    text_kv,
    active,
    counts,
    hidden,
    w_out,
    mod_shift,
    mod_scale,
    w_final,
    latent,
    cached_velocity,
    step_size,
):
    groups = lax.axis_size("head")
    planes = lax.axis_size("zb")
    block = lax.axis_index("zb")
    own = lax.axis_index(SEQ)
    slots = query.shape[0]
    tokens = cache_kv.shape[1]
    near_axes = ("za", "y")
    copies = lax.axis_size(near_axes)

    info = jnp.stack([own * tokens, counts[0]]).astype(jnp.int32)
    pos = active.reshape(1, slots)
    gathered = lax.all_gather(query, "zb", axis=0, tiled=True)
    filled = fill(info, pos, new_kv, cache_kv, copies)
    near = lax.all_to_all(filled, near_axes, 0, 0, tiled=True)
    far = lax.ppermute(near, "core", [(0, 1), (1, 0)])
    part = block.reshape(1).astype(jnp.int32)
    partial = attend(part, planes, gathered, near, far, text_kv, slots, 192)
    returned = lax.all_to_all(partial, "zb", 0, 0, tiled=True)
    terms = merge(returned, w_out, groups)
    terms = lax.all_to_all(terms, "head", 0, 0, tiled=True)
    stats = norm(
        terms, hidden, mod_scale.reshape(1, -1), mod_shift.reshape(1, -1), w_final
    )
    stats = lax.all_to_all(stats, "head", 0, 0, tiled=True)
    return finish(info, step_size, pos, stats, latent, cached_velocity)


def solution(mesh):
    in_specs = (
        P(SEQ, "head"),
        P(None, SEQ, "head"),
        P(None, SEQ, "head"),
        P(None, None, "head"),
        P(SEQ),
        P(SEQ),
        P(SEQ, "head"),
        P("head", None),
        P("head"),
        P("head"),
        P("head", None),
        P(SEQ, None),
        P(SEQ, None),
        P(),
    )
    out_specs = (P(SEQ, None), P(SEQ, None))
    split = jax.sharding.Mesh(
        mesh.devices.reshape(8, 2, 4, 2, mesh.shape["head"]), SEQ + ("head",)
    )

    return jax.shard_map(
        on_device, mesh=split, in_specs=in_specs, out_specs=out_specs, check_vma=False
    )
```

```python
import functools

import jax
import jax.numpy as jnp
from jax import lax
from jax.experimental import pallas as pl
from jax.experimental.pallas import tpu as pltpu
from jax.sharding import PartitionSpec as P


D = 3072
HD = 128
EPS = 1e-06
LOG2E = 1.4426950408889634
SCALE = HD ** (-0.5)
SEQ = ("zh", "zl", "y", "core")
STAT = 8


f32 = jnp.float32
bf16 = jnp.bfloat16
VM = pl.BlockSpec(memory_space=pltpu.VMEM)
SM = pl.BlockSpec(memory_space=pltpu.SMEM)


def one_hot(pos_ref, info_ref, rows, cols):
    local = pos_ref[...] - info_ref[0]
    slot = lax.broadcasted_iota(jnp.int32, (1, cols), 1)
    local = jnp.where(slot < info_ref[1], local, -1)
    return lax.broadcasted_iota(jnp.int32, (rows, cols), 0) == local


def fill_kernel(info_ref, pos_ref, new_ref, cache_ref, out_ref):
    rows, cols = cache_ref.shape[1], new_ref.shape[1]
    matched = one_hot(pos_ref, info_ref, rows, cols)
    pick = matched.astype(f32)
    keep = jnp.max(pick, axis=1, keepdims=True) < 0.5
    pick = pick.astype(bf16)
    for s in range(2):
        placed = jnp.dot(pick, new_ref[s], preferred_element_type=f32)
        merged = jnp.where(keep, cache_ref[s].astype(f32), placed).astype(bf16)
        out_ref[s] = merged


def fill(info, pos, new_kv, cache_kv):
    return pl.pallas_call(
        fill_kernel,
        out_shape=jax.ShapeDtypeStruct(cache_kv.shape, bf16),
        in_specs=[SM, VM, VM, VM],
        out_specs=VM,
    )(info, pos, new_kv, cache_kv)


def attend_kernel(part_ref, q_ref, a_ref, b_ref, t_ref, out_ref, *, chunk):
    del part_ref
    slots = out_ref.shape[1] - STAT
    keys, values = [], []
    for ref in (a_ref, b_ref):
        n = ref.shape[0] * ref.shape[2]
        keys.append(ref[:, 0].reshape(n, HD))
        values.append(ref[:, 1].reshape(n, HD))
    keys.append(t_ref[0])
    values.append(t_ref[1])
    lane = lax.broadcasted_iota(jnp.int32, (slots, HD), 1)
    eye = lax.broadcasted_iota(jnp.int32, (slots, HD), 0) == lane
    row = lax.broadcasted_iota(jnp.int32, (STAT, HD), 0)
    for start in range(0, q_ref.shape[0], chunk):
        q = q_ref[pl.ds(start, chunk), :]
        scores = [
            lax.dot_general(q, k, (((1,), (1,)), ((), ())), preferred_element_type=f32)
            for k in keys
        ]
        top = functools.reduce(
            jnp.maximum, [jnp.max(s, axis=1, keepdims=True) for s in scores]
        )
        weights = [jnp.exp2((s - top) * (SCALE * LOG2E)) for s in scores]
        total = sum(jnp.sum(w, axis=1, keepdims=True) for w in weights)
        mixed = sum(
            jnp.dot(w.astype(bf16), v, preferred_element_type=f32)
            for w, v in zip(weights, values)
        )
        mixed = mixed / total
        spread = top * SCALE + jnp.log(total)
        for i in range(chunk // slots):
            d = start // slots + i
            out_ref[d, 0:slots, :] = mixed[i * slots : (i + 1) * slots].astype(bf16)
            column = spread[i * slots : (i + 1) * slots]
            line = jnp.sum(jnp.where(eye, column, 0.0), axis=0, keepdims=True)
            first = line.astype(bf16).astype(f32)
            second = (line - first).astype(bf16).astype(f32)
            third = line - first - second
            pieces = jnp.where(row == 0, first, jnp.where(row == 1, second, third))
            out_ref[d, slots : slots + STAT, :] = pieces.astype(bf16)


def attend(part, parts, queries, near, far, text_kv, slots, chunk):
    rows, width = queries.shape
    text_rows = text_kv.shape[1] // parts
    kv_spec = pl.BlockSpec(near.shape[:3] + (HD,), lambda h, part: (0, 0, 0, h))
    return pl.pallas_call(
        functools.partial(attend_kernel, chunk=chunk),
        out_shape=jax.ShapeDtypeStruct((parts, slots + STAT, width), bf16),
        grid_spec=pltpu.PrefetchScalarGridSpec(
            num_scalar_prefetch=1,
            grid=(width // HD,),
            in_specs=[
                pl.BlockSpec((rows, HD), lambda h, part: (0, h)),
                kv_spec,
                kv_spec,
                pl.BlockSpec((2, text_rows, HD), lambda h, part: (0, part[0], h)),
            ],
            out_specs=pl.BlockSpec((parts, slots + STAT, HD), lambda h, part: (0, 0, h)),
        ),
    )(part, queries, near, far, text_kv)


def merge_kernel(got_ref, w_ref, out_ref):
    parts, rows, width = got_ref.shape
    slots = rows - STAT
    heads = []
    for h in range(width // HD):
        cols = slice(h * HD, (h + 1) * HD)
        stat = got_ref[:, slots:rows, cols].astype(f32)
        spread = stat[:, 0] + stat[:, 1] + stat[:, 2]
        share = jnp.exp(spread - jnp.max(spread, axis=0, keepdims=True))
        share = share / jnp.sum(share, axis=0, keepdims=True)
        share = jnp.concatenate([share, jnp.zeros((HD - parts, HD), f32)], axis=0).T
        total = jnp.zeros((slots, HD), f32)
        for s in range(parts):
            total += got_ref[s, 0:slots, cols].astype(f32) * share[0:slots, s : s + 1]
        heads.append(total.astype(bf16))
    attended = jnp.concatenate(heads, axis=1)
    piece = out_ref.shape[2]
    for k in range(out_ref.shape[0]):
        out_ref[k] = jnp.dot(
            attended, w_ref[:, k * piece : (k + 1) * piece], preferred_element_type=f32
        ).astype(bf16)


def merge(got, w_out, groups):
    return pl.pallas_call(
        merge_kernel,
        out_shape=jax.ShapeDtypeStruct(
            (groups, got.shape[1] - STAT, w_out.shape[1] // groups), bf16
        ),
        in_specs=[VM, VM],
        out_specs=VM,
    )(got, w_out)


def norm_kernel(got_ref, hidden_ref, scale_ref, shift_ref, w_ref, out_ref):
    slots, width = hidden_ref.shape
    summed = hidden_ref[...].astype(f32)
    for k in range(got_ref.shape[0]):
        summed += got_ref[k].astype(f32)
    mean = jnp.sum(summed, axis=1, keepdims=True) * (1.0 / width)
    centred = summed - mean
    squares = jnp.sum(centred * centred, axis=1, keepdims=True)
    lifted = 1.0 + scale_ref[...]
    tail = lax.broadcasted_iota(jnp.int32, (STAT, width), 0)
    tail = jnp.where(tail == 0, lifted, jnp.where(tail == 1, shift_ref[...], 0.0))
    rows = jnp.concatenate([centred * lifted, tail], axis=0)
    mapped = lax.dot_general(
        rows,
        w_ref[...],
        (((1,), (1,)), ((), ())),
        precision=lax.Precision.HIGHEST,
        preferred_element_type=f32,
    )
    lane = lax.broadcasted_iota(jnp.int32, (slots, 64), 1)
    stat = jnp.where(lane == 0, mean, jnp.where(lane == 1, squares, 0.0))
    stat = jnp.concatenate([stat, jnp.zeros((STAT, 64), f32)], axis=0)
    block = jnp.concatenate([mapped, stat], axis=1)
    for k in range(out_ref.shape[0]):
        out_ref[k] = block


def norm(got, hidden, scale, shift, w_final):
    return pl.pallas_call(
        norm_kernel,
        out_shape=jax.ShapeDtypeStruct(
            (got.shape[0], hidden.shape[0] + STAT, 2 * w_final.shape[1]), f32
        ),
        in_specs=[VM] * 5,
        out_specs=VM,
    )(got, hidden, scale, shift, w_final.T)


def finish_kernel(
    info_ref, step_ref, pos_ref, got_ref, latent_ref, old_ref, velocity_ref, next_ref
):
    groups, rows, _ = got_ref.shape
    slots = rows - STAT
    ch = latent_ref.shape[0]
    blocks = [got_ref[k] for k in range(groups)]
    means = [b[0:slots, ch : ch + 1] for b in blocks]
    mean = sum(means) * (1.0 / groups)
    width = D // groups
    var = sum(b[0:slots, ch + 1 : ch + 2] for b in blocks)
    var = (var + width * sum((m - mean) * (m - mean) for m in means)) * (1.0 / D)
    mapped = sum(
        b[0:slots, 0:ch] + (m - mean) * b[slots : slots + 1, 0:ch]
        for b, m in zip(blocks, means)
    )
    base = sum(b[slots + 1 : slots + 2, 0:ch] for b in blocks)
    fresh = mapped * lax.rsqrt(var + EPS) + base
    tokens = latent_ref.shape[1]
    pick = one_hot(pos_ref, info_ref, tokens, slots).astype(f32)
    keep = lax.dot_general(
        jnp.ones((8, slots), f32),
        pick,
        (((1,), (1,)), ((), ())),
        preferred_element_type=f32,
    )[0:1]
    chosen = lax.dot_general(
        fresh,
        pick,
        (((0,), (1,)), ((), ())),
        precision=lax.Precision.HIGHEST,
        preferred_element_type=f32,
    )
    velocity = jnp.where(keep < 0.5, old_ref[...], chosen)
    velocity_ref[...] = velocity
    next_ref[...] = latent_ref[...] + step_ref[0] * velocity


def finish(info, step_size, pos, got, latent, cached_velocity):
    velocity, following = pl.pallas_call(
        finish_kernel,
        out_shape=(
            jax.ShapeDtypeStruct(latent.shape[::-1], f32),
            jax.ShapeDtypeStruct(latent.shape[::-1], f32),
        ),
        in_specs=[SM, SM, VM, VM, VM, VM],
        out_specs=(VM, VM),
    )(info, step_size, pos, got, latent.T, cached_velocity.T)
    return velocity.T, following.T


def on_device(
    query,
    new_kv,
    cache_kv,
    text_kv,
    active,
    counts,
    hidden,
    w_out,
    mod_shift,
    mod_scale,
    w_final,
    latent,
    cached_velocity,
    step_size,
):
    groups = lax.axis_size("head")
    around = ("zl", "y")
    parts = lax.axis_size(around)
    own = lax.axis_index(SEQ)
    slots = query.shape[0]
    tokens = cache_kv.shape[1]

    info = jnp.stack([own * tokens, counts[0]]).astype(jnp.int32)
    pos = active.reshape(1, slots)
    filled = fill(info, pos, new_kv, cache_kv)
    near = lax.all_gather(filled, "zh", axis=0, tiled=False)
    far = lax.ppermute(near, "core", [(0, 1), (1, 0)])
    asked = jnp.broadcast_to(query[None], (parts,) + query.shape)
    gathered = lax.all_to_all(asked, around, 0, 0, tiled=True)
    gathered = gathered.reshape(parts * slots, -1)
    part = lax.axis_index(around).reshape(1).astype(jnp.int32)
    partial = attend(part, parts, gathered, near, far, text_kv, slots, 192)
    returned = lax.all_to_all(partial, around, 0, 0, tiled=True)
    terms = merge(returned, w_out, groups)
    terms = lax.all_to_all(terms, "head", 0, 0, tiled=True)
    stats = norm(
        terms, hidden, mod_scale.reshape(1, -1), mod_shift.reshape(1, -1), w_final
    )
    stats = lax.all_to_all(stats, "head", 0, 0, tiled=True)
    return finish(info, step_size, pos, stats, latent, cached_velocity)


def solution(mesh):
    in_specs = (
        P(SEQ, "head"),
        P(None, SEQ, "head"),
        P(None, SEQ, "head"),
        P(None, None, "head"),
        P(SEQ),
        P(SEQ),
        P(SEQ, "head"),
        P("head", None),
        P("head"),
        P("head"),
        P("head", None),
        P(SEQ, None),
        P(SEQ, None),
        P(),
    )
    out_specs = (P(SEQ, None), P(SEQ, None))
    split = jax.sharding.Mesh(
        mesh.devices.reshape(4, 4, 4, 2, mesh.shape["head"]), SEQ + ("head",)
    )

    return jax.shard_map(
        on_device, mesh=split, in_specs=in_specs, out_specs=out_specs, check_vma=False
    )
```

```python
import functools

import jax
import jax.numpy as jnp
from jax import lax
from jax.experimental import pallas as pl
from jax.experimental.pallas import tpu as pltpu
from jax.sharding import PartitionSpec as P


D = 3072
HD = 128
EPS = 1e-06
LOG2E = 1.4426950408889634
SCALE = HD ** (-0.5)
SEQ = ("zh", "zl", "y", "core")
STAT = 8


f32 = jnp.float32
bf16 = jnp.bfloat16
VM = pl.BlockSpec(memory_space=pltpu.VMEM)


def one_hot(pos_ref, count_ref, rows, cols):
    local = pos_ref[...] - lax.axis_index(SEQ) * rows
    slot = lax.broadcasted_iota(jnp.int32, (1, cols), 1)
    local = jnp.where(slot < count_ref[...], local, -1)
    return lax.broadcasted_iota(jnp.int32, (rows, cols), 0) == local


def fill_kernel(
    count_ref, step_ref, pos_ref, q_ref, new_ref, cache_ref, out_ref, asked_ref, row_ref
):
    rows, cols = cache_ref.shape[1], new_ref.shape[1]
    matched = one_hot(pos_ref, count_ref, rows, cols)
    pick = matched.astype(f32)
    keep = jnp.max(pick, axis=1, keepdims=True) < 0.5
    pick = pick.astype(bf16)
    for s in range(2):
        placed = jnp.dot(pick, new_ref[s], preferred_element_type=f32)
        merged = jnp.where(keep, cache_ref[s].astype(f32), placed).astype(bf16)
        out_ref[s] = merged
    for d in range(asked_ref.shape[0]):
        asked_ref[d] = q_ref[...]
    row_ref[...] = jnp.broadcast_to(step_ref[...], row_ref.shape)


def fill(count, step_size, pos, query, new_kv, cache_kv, copies):
    return pl.pallas_call(
        fill_kernel,
        out_shape=(
            jax.ShapeDtypeStruct(cache_kv.shape, bf16),
            jax.ShapeDtypeStruct((copies,) + query.shape, bf16),
            jax.ShapeDtypeStruct((8, 128), f32),
        ),
        in_specs=[VM] * 6,
        out_specs=(VM, VM, VM),
    )(count, step_size, pos, query, new_kv, cache_kv)


def touch_kernel(in_ref, out_ref):
    del in_ref, out_ref


def touch(x):
    any_space = pl.BlockSpec(memory_space=pl.ANY)
    return pl.pallas_call(
        touch_kernel,
        out_shape=jax.ShapeDtypeStruct(x.shape, x.dtype),
        in_specs=[any_space],
        out_specs=any_space,
        input_output_aliases={0: 0},
    )(x)


def attend_kernel(q_ref, a_ref, b_ref, t_ref, out_ref, *, chunk, around):
    slots = out_ref.shape[1] - STAT
    keys, values = [], []
    for ref in (a_ref, b_ref):
        n = ref.shape[0] * ref.shape[2]
        keys.append(ref[:, 0].reshape(n, HD))
        values.append(ref[:, 1].reshape(n, HD))
    share = t_ref.shape[1] // out_ref.shape[0]
    own_text = pl.ds(pl.multiple_of(lax.axis_index(around) * share, share), share)
    keys.append(t_ref[0, own_text, :])
    values.append(t_ref[1, own_text, :])
    lane = lax.broadcasted_iota(jnp.int32, (slots, HD), 1)
    eye = lax.broadcasted_iota(jnp.int32, (slots, HD), 0) == lane
    row = lax.broadcasted_iota(jnp.int32, (STAT, HD), 0)
    for start in range(0, q_ref.shape[0], chunk):
        q = q_ref[pl.ds(start, chunk), :]
        scores = [
            lax.dot_general(q, k, (((1,), (1,)), ((), ())), preferred_element_type=f32)
            for k in keys
        ]
        top = functools.reduce(
            jnp.maximum, [jnp.max(s, axis=1, keepdims=True) for s in scores]
        )
        weights = [jnp.exp2((s - top) * (SCALE * LOG2E)) for s in scores]
        total = sum(jnp.sum(w, axis=1, keepdims=True) for w in weights)
        mixed = sum(
            jnp.dot(w.astype(bf16), v, preferred_element_type=f32)
            for w, v in zip(weights, values)
        )
        mixed = mixed / total
        spread = top * SCALE + jnp.log(total)
        for i in range(chunk // slots):
            d = start // slots + i
            out_ref[d, 0:slots, :] = mixed[i * slots : (i + 1) * slots].astype(bf16)
            column = spread[i * slots : (i + 1) * slots]
            line = jnp.sum(jnp.where(eye, column, 0.0), axis=0, keepdims=True)
            first = line.astype(bf16).astype(f32)
            second = (line - first).astype(bf16).astype(f32)
            third = line - first - second
            pieces = jnp.where(row == 0, first, jnp.where(row == 1, second, third))
            out_ref[d, slots : slots + STAT, :] = pieces.astype(bf16)


def attend(parts, around, queries, near, far, text_kv, slots, chunk):
    rows, width = queries.shape
    kv_spec = pl.BlockSpec(near.shape[:3] + (HD,), lambda h: (0, 0, 0, h))
    return pl.pallas_call(
        functools.partial(attend_kernel, chunk=chunk, around=around),
        out_shape=jax.ShapeDtypeStruct((parts, slots + STAT, width), bf16),
        grid=(width // HD,),
        in_specs=[
            pl.BlockSpec((rows, HD), lambda h: (0, h)),
            kv_spec,
            kv_spec,
            pl.BlockSpec(text_kv.shape[:2] + (HD,), lambda h: (0, 0, h)),
        ],
        out_specs=pl.BlockSpec((parts, slots + STAT, HD), lambda h: (0, 0, h)),
    )(queries, near, far, text_kv)


def merge_kernel(got_ref, w_ref, out_ref):
    parts, rows, width = got_ref.shape
    slots = rows - STAT
    heads = []
    for h in range(width // HD):
        cols = slice(h * HD, (h + 1) * HD)
        stat = got_ref[:, slots:rows, cols].astype(f32)
        spread = stat[:, 0] + stat[:, 1] + stat[:, 2]
        share = jnp.exp(spread - jnp.max(spread, axis=0, keepdims=True))
        share = share / jnp.sum(share, axis=0, keepdims=True)
        share = jnp.concatenate([share, jnp.zeros((HD - parts, HD), f32)], axis=0).T
        total = jnp.zeros((slots, HD), f32)
        for s in range(parts):
            total += got_ref[s, 0:slots, cols].astype(f32) * share[0:slots, s : s + 1]
        heads.append(total.astype(bf16))
    attended = jnp.concatenate(heads, axis=1)
    piece = out_ref.shape[2]
    for k in range(out_ref.shape[0]):
        out_ref[k] = jnp.dot(
            attended, w_ref[:, k * piece : (k + 1) * piece], preferred_element_type=f32
        ).astype(bf16)


def merge(got, w_out, groups):
    return pl.pallas_call(
        merge_kernel,
        out_shape=jax.ShapeDtypeStruct(
            (groups, got.shape[1] - STAT, w_out.shape[1] // groups), bf16
        ),
        in_specs=[VM, VM],
        out_specs=VM,
    )(got, w_out)


def flat(ref):
    return jnp.concatenate([ref[i : i + 1, :] for i in range(ref.shape[0])], axis=1)


def norm_kernel(got_ref, hidden_ref, scale_ref, shift_ref, w_ref, out_ref):
    slots, width = hidden_ref.shape
    summed = hidden_ref[...].astype(f32)
    for k in range(got_ref.shape[0]):
        summed += got_ref[k].astype(f32)
    mean = jnp.sum(summed, axis=1, keepdims=True) * (1.0 / width)
    centred = summed - mean
    squares = jnp.sum(centred * centred, axis=1, keepdims=True)
    lifted = 1.0 + flat(scale_ref)
    tail = lax.broadcasted_iota(jnp.int32, (STAT, width), 0)
    tail = jnp.where(tail == 0, lifted, jnp.where(tail == 1, flat(shift_ref), 0.0))
    rows = jnp.concatenate([centred * lifted, tail], axis=0)
    mapped = lax.dot_general(
        rows,
        w_ref[...],
        (((1,), (1,)), ((), ())),
        precision=lax.Precision.HIGHEST,
        preferred_element_type=f32,
    )
    lane = lax.broadcasted_iota(jnp.int32, (slots, 64), 1)
    stat = jnp.where(lane == 0, mean, jnp.where(lane == 1, squares, 0.0))
    stat = jnp.concatenate([stat, jnp.zeros((STAT, 64), f32)], axis=0)
    block = jnp.concatenate([mapped, stat], axis=1)
    for k in range(out_ref.shape[0]):
        out_ref[k] = block


def norm(got, hidden, scale, shift, w_final):
    return pl.pallas_call(
        norm_kernel,
        out_shape=jax.ShapeDtypeStruct(
            (got.shape[0], hidden.shape[0] + STAT, 2 * w_final.shape[1]), f32
        ),
        in_specs=[VM] * 5,
        out_specs=VM,
    )(got, hidden, scale, shift, w_final.T)


def finish_kernel(
    count_ref, step_ref, pos_ref, got_ref, latent_ref, old_ref, velocity_ref, next_ref
):
    groups, rows, _ = got_ref.shape
    slots = rows - STAT
    ch = latent_ref.shape[0]
    blocks = [got_ref[k] for k in range(groups)]
    means = [b[0:slots, ch : ch + 1] for b in blocks]
    mean = sum(means) * (1.0 / groups)
    width = D // groups
    var = sum(b[0:slots, ch + 1 : ch + 2] for b in blocks)
    var = (var + width * sum((m - mean) * (m - mean) for m in means)) * (1.0 / D)
    mapped = sum(
        b[0:slots, 0:ch] + (m - mean) * b[slots : slots + 1, 0:ch]
        for b, m in zip(blocks, means)
    )
    base = sum(b[slots + 1 : slots + 2, 0:ch] for b in blocks)
    fresh = mapped * lax.rsqrt(var + EPS) + base
    tokens = latent_ref.shape[1]
    pick = one_hot(pos_ref, count_ref, tokens, slots).astype(f32)
    keep = lax.dot_general(
        jnp.ones((8, slots), f32),
        pick,
        (((1,), (1,)), ((), ())),
        preferred_element_type=f32,
    )[0:1]
    chosen = lax.dot_general(
        fresh,
        pick,
        (((0,), (1,)), ((), ())),
        precision=lax.Precision.HIGHEST,
        preferred_element_type=f32,
    )
    velocity = jnp.where(keep < 0.5, old_ref[...], chosen)
    velocity_ref[...] = velocity
    next_ref[...] = latent_ref[...] + step_ref[0:1, :] * velocity


def finish(count, step_size, pos, got, latent, cached_velocity):
    velocity, following = pl.pallas_call(
        finish_kernel,
        out_shape=(
            jax.ShapeDtypeStruct(latent.shape[::-1], f32),
            jax.ShapeDtypeStruct(latent.shape[::-1], f32),
        ),
        in_specs=[VM] * 6,
        out_specs=(VM, VM),
    )(count, step_size, pos, got, latent.T, cached_velocity.T)
    return velocity.T, following.T


def on_device(
    query,
    new_kv,
    cache_kv,
    text_kv,
    active,
    counts,
    hidden,
    w_out,
    mod_shift,
    mod_scale,
    w_final,
    latent,
    cached_velocity,
    step_size,
):
    groups = lax.axis_size("head")
    around = ("zl", "y")
    parts = lax.axis_size(around)
    slots = query.shape[0]

    count = counts.reshape(1, 1)
    pos = active.reshape(1, slots)
    filled, asked, step_row = fill(
        count, step_size.reshape(1, 1), pos, query, new_kv, cache_kv, parts
    )
    near = lax.all_gather(filled, "zh", axis=0, tiled=False)
    far = lax.ppermute(near, "core", [(0, 1), (1, 0)])
    gathered = lax.all_to_all(asked, around, 0, 0, tiled=True)
    gathered = touch(gathered)
    gathered = gathered.reshape(parts * slots, -1)
    partial = attend(parts, around, gathered, near, far, text_kv, slots, 192)
    returned = lax.all_to_all(partial, around, 0, 0, tiled=True)
    terms = merge(returned, w_out, groups)
    terms = lax.all_to_all(terms, "head", 0, 0, tiled=True)
    stats = norm(
        terms, hidden, mod_scale.reshape(-1, 128), mod_shift.reshape(-1, 128), w_final
    )
    stats = lax.all_to_all(stats, "head", 0, 0, tiled=True)
    return finish(count, step_row, pos, stats, latent, cached_velocity)


def solution(mesh):
    in_specs = (
        P(SEQ, "head"),
        P(None, SEQ, "head"),
        P(None, SEQ, "head"),
        P(None, None, "head"),
        P(SEQ),
        P(SEQ),
        P(SEQ, "head"),
        P("head", None),
        P("head"),
        P("head"),
        P("head", None),
        P(SEQ, None),
        P(SEQ, None),
        P(),
    )
    out_specs = (P(SEQ, None), P(SEQ, None))
    split = jax.sharding.Mesh(
        mesh.devices.reshape(4, 4, 4, 2, mesh.shape["head"]), SEQ + ("head",)
    )

    return jax.shard_map(
        on_device, mesh=split, in_specs=in_specs, out_specs=out_specs, check_vma=False
    )
```

```python
import functools

import jax
import jax.numpy as jnp
from jax import lax
from jax.experimental import pallas as pl
from jax.experimental.pallas import tpu as pltpu
from jax.sharding import PartitionSpec as P


D = 3072
HD = 128
EPS = 1e-06
LOG2E = 1.4426950408889634
SCALE = HD ** (-0.5)
SEQ = ("zh", "zl", "y", "core")
STAT = 8


f32 = jnp.float32
bf16 = jnp.bfloat16
VM = pl.BlockSpec(memory_space=pltpu.VMEM)


def grant(mebibytes):
    return pltpu.CompilerParams(vmem_limit_bytes=mebibytes * 2**20)


def local(*arrays):
    return [pltpu.with_memory_space_constraint(x, pltpu.VMEM) for x in arrays]


def one_hot(pos_ref, count_ref, rows, cols):
    local = pos_ref[...] - lax.axis_index(SEQ) * rows
    slot = lax.broadcasted_iota(jnp.int32, (1, cols), 1)
    local = jnp.where(slot < count_ref[...], local, -1)
    return lax.broadcasted_iota(jnp.int32, (rows, cols), 0) == local


def fill_kernel(
    count_ref, step_ref, pos_ref, q_ref, new_ref, cache_ref, out_ref, asked_ref, row_ref
):
    rows, cols = cache_ref.shape[1], new_ref.shape[1]
    matched = one_hot(pos_ref, count_ref, rows, cols)
    pick = matched.astype(f32)
    keep = jnp.max(pick, axis=1, keepdims=True) < 0.5
    pick = pick.astype(bf16)
    for s in range(2):
        placed = jnp.dot(pick, new_ref[s], preferred_element_type=f32)
        merged = jnp.where(keep, cache_ref[s].astype(f32), placed).astype(bf16)
        out_ref[s] = merged
    for d in range(asked_ref.shape[0]):
        asked_ref[d] = q_ref[...]
    row_ref[...] = jnp.broadcast_to(step_ref[...], row_ref.shape)


def fill(count, step_size, pos, query, new_kv, cache_kv, copies):
    return pl.pallas_call(
        fill_kernel,
        out_shape=(
            pltpu.VMEM(cache_kv.shape, bf16),
            pltpu.VMEM((copies,) + query.shape, bf16),
            pltpu.VMEM((8, 128), f32),
        ),
        in_specs=[VM] * 6,
        out_specs=(VM, VM, VM),
        compiler_params=grant(8),
    )(count, step_size, pos, query, new_kv, cache_kv)


def touch_kernel(in_ref, out_ref):
    del in_ref, out_ref


def touch(x):
    return pl.pallas_call(
        touch_kernel,
        out_shape=pltpu.VMEM(x.shape, x.dtype),
        in_specs=[VM],
        out_specs=VM,
        input_output_aliases={0: 0},
        compiler_params=grant(2),
    )(*local(x))


def attend_kernel(q_ref, a_ref, b_ref, t_ref, out_ref, *, chunk, around):
    slots = out_ref.shape[1] - STAT
    share = t_ref.shape[1] // out_ref.shape[0]
    own_text = pl.ds(pl.multiple_of(lax.axis_index(around) * share, share), share)
    lane = lax.broadcasted_iota(jnp.int32, (slots, HD), 1)
    eye = lax.broadcasted_iota(jnp.int32, (slots, HD), 0) == lane
    row = lax.broadcasted_iota(jnp.int32, (STAT, HD), 0)
    for h in range(q_ref.shape[1] // HD):
        cols = slice(h * HD, (h + 1) * HD)
        keys, values = [], []
        for ref in (a_ref, b_ref):
            n = ref.shape[0] * ref.shape[2]
            keys.append(ref[:, 0, :, cols].reshape(n, HD))
            values.append(ref[:, 1, :, cols].reshape(n, HD))
        keys.append(t_ref[0, own_text, cols])
        values.append(t_ref[1, own_text, cols])
        for start in range(0, q_ref.shape[0], chunk):
            q = q_ref[pl.ds(start, chunk), cols]
            scores = [
                lax.dot_general(
                    q, k, (((1,), (1,)), ((), ())), preferred_element_type=f32
                )
                for k in keys
            ]
            top = functools.reduce(
                jnp.maximum, [jnp.max(s, axis=1, keepdims=True) for s in scores]
            )
            weights = [jnp.exp2((s - top) * (SCALE * LOG2E)) for s in scores]
            total = sum(jnp.sum(w, axis=1, keepdims=True) for w in weights)
            mixed = sum(
                jnp.dot(w.astype(bf16), v, preferred_element_type=f32)
                for w, v in zip(weights, values)
            )
            mixed = mixed / total
            spread = top * SCALE + jnp.log(total)
            for i in range(chunk // slots):
                d = start // slots + i
                part = slice(i * slots, (i + 1) * slots)
                out_ref[d, 0:slots, cols] = mixed[part].astype(bf16)
                line = jnp.sum(
                    jnp.where(eye, spread[part], 0.0), axis=0, keepdims=True
                )
                first = line.astype(bf16).astype(f32)
                second = (line - first).astype(bf16).astype(f32)
                third = line - first - second
                pieces = jnp.where(row == 0, first, jnp.where(row == 1, second, third))
                out_ref[d, slots : slots + STAT, cols] = pieces.astype(bf16)


def attend(parts, around, queries, near, far, text_kv, slots, chunk):
    return pl.pallas_call(
        functools.partial(attend_kernel, chunk=chunk, around=around),
        out_shape=pltpu.VMEM((parts, slots + STAT, queries.shape[1]), bf16),
        in_specs=[VM] * 4,
        out_specs=VM,
        compiler_params=grant(20),
    )(*local(queries, near, far, text_kv))


def merge_kernel(got_ref, w_ref, out_ref):
    parts, rows, width = got_ref.shape
    slots = rows - STAT
    heads = []
    for h in range(width // HD):
        cols = slice(h * HD, (h + 1) * HD)
        stat = got_ref[:, slots:rows, cols].astype(f32)
        spread = stat[:, 0] + stat[:, 1] + stat[:, 2]
        share = jnp.exp(spread - jnp.max(spread, axis=0, keepdims=True))
        share = share / jnp.sum(share, axis=0, keepdims=True)
        share = jnp.concatenate([share, jnp.zeros((HD - parts, HD), f32)], axis=0).T
        total = jnp.zeros((slots, HD), f32)
        for s in range(parts):
            total += got_ref[s, 0:slots, cols].astype(f32) * share[0:slots, s : s + 1]
        heads.append(total.astype(bf16))
    attended = jnp.concatenate(heads, axis=1)
    piece = out_ref.shape[2]
    for k in range(out_ref.shape[0]):
        out_ref[k] = jnp.dot(
            attended, w_ref[:, k * piece : (k + 1) * piece], preferred_element_type=f32
        ).astype(bf16)


def merge(got, w_out, groups):
    return pl.pallas_call(
        merge_kernel,
        out_shape=pltpu.VMEM(
            (groups, got.shape[1] - STAT, w_out.shape[1] // groups), bf16
        ),
        in_specs=[VM, VM],
        out_specs=VM,
        compiler_params=grant(8),
    )(*local(got, w_out))


def flat(ref):
    return jnp.concatenate([ref[i : i + 1, :] for i in range(ref.shape[0])], axis=1)


def norm_kernel(got_ref, hidden_ref, scale_ref, shift_ref, w_ref, out_ref):
    slots, width = hidden_ref.shape
    summed = hidden_ref[...].astype(f32)
    for k in range(got_ref.shape[0]):
        summed += got_ref[k].astype(f32)
    mean = jnp.sum(summed, axis=1, keepdims=True) * (1.0 / width)
    centred = summed - mean
    squares = jnp.sum(centred * centred, axis=1, keepdims=True)
    lifted = 1.0 + flat(scale_ref)
    tail = lax.broadcasted_iota(jnp.int32, (STAT, width), 0)
    tail = jnp.where(tail == 0, lifted, jnp.where(tail == 1, flat(shift_ref), 0.0))
    rows = jnp.concatenate([centred * lifted, tail], axis=0)
    mapped = lax.dot_general(
        rows,
        w_ref[...],
        (((1,), (1,)), ((), ())),
        precision=lax.Precision.HIGHEST,
        preferred_element_type=f32,
    )
    lane = lax.broadcasted_iota(jnp.int32, (slots, 64), 1)
    stat = jnp.where(lane == 0, mean, jnp.where(lane == 1, squares, 0.0))
    stat = jnp.concatenate([stat, jnp.zeros((STAT, 64), f32)], axis=0)
    block = jnp.concatenate([mapped, stat], axis=1)
    for k in range(out_ref.shape[0]):
        out_ref[k] = block


def norm(got, hidden, scale, shift, w_final):
    return pl.pallas_call(
        norm_kernel,
        out_shape=pltpu.VMEM(
            (got.shape[0], hidden.shape[0] + STAT, 2 * w_final.shape[1]), f32
        ),
        in_specs=[VM] * 5,
        out_specs=VM,
        compiler_params=grant(8),
    )(*local(got, hidden, scale, shift, w_final.T))


def finish_kernel(
    count_ref, step_ref, pos_ref, got_ref, latent_ref, old_ref, velocity_ref, next_ref
):
    groups, rows, _ = got_ref.shape
    slots = rows - STAT
    ch = latent_ref.shape[0]
    blocks = [got_ref[k] for k in range(groups)]
    means = [b[0:slots, ch : ch + 1] for b in blocks]
    mean = sum(means) * (1.0 / groups)
    width = D // groups
    var = sum(b[0:slots, ch + 1 : ch + 2] for b in blocks)
    var = (var + width * sum((m - mean) * (m - mean) for m in means)) * (1.0 / D)
    mapped = sum(
        b[0:slots, 0:ch] + (m - mean) * b[slots : slots + 1, 0:ch]
        for b, m in zip(blocks, means)
    )
    base = sum(b[slots + 1 : slots + 2, 0:ch] for b in blocks)
    fresh = mapped * lax.rsqrt(var + EPS) + base
    tokens = latent_ref.shape[1]
    pick = one_hot(pos_ref, count_ref, tokens, slots).astype(f32)
    keep = lax.dot_general(
        jnp.ones((8, slots), f32),
        pick,
        (((1,), (1,)), ((), ())),
        preferred_element_type=f32,
    )[0:1]
    chosen = lax.dot_general(
        fresh,
        pick,
        (((0,), (1,)), ((), ())),
        precision=lax.Precision.HIGHEST,
        preferred_element_type=f32,
    )
    velocity = jnp.where(keep < 0.5, old_ref[...], chosen)
    velocity_ref[...] = velocity
    next_ref[...] = latent_ref[...] + step_ref[0:1, :] * velocity


def finish(count, step_size, pos, got, latent, cached_velocity):
    velocity, following = pl.pallas_call(
        finish_kernel,
        out_shape=(
            jax.ShapeDtypeStruct(latent.shape[::-1], f32),
            jax.ShapeDtypeStruct(latent.shape[::-1], f32),
        ),
        in_specs=[VM] * 6,
        out_specs=(VM, VM),
        compiler_params=grant(8),
    )(count, *local(step_size), pos, *local(got, latent.T, cached_velocity.T))
    return velocity.T, following.T


def on_device(
    query,
    new_kv,
    cache_kv,
    text_kv,
    active,
    counts,
    hidden,
    w_out,
    mod_shift,
    mod_scale,
    w_final,
    latent,
    cached_velocity,
    step_size,
):
    groups = lax.axis_size("head")
    around = ("zl", "y")
    parts = lax.axis_size(around)
    slots = query.shape[0]

    count = counts.reshape(1, 1)
    pos = active.reshape(1, slots)
    filled, asked, step_row = fill(
        count, step_size.reshape(1, 1), pos, query, new_kv, cache_kv, parts
    )
    near = lax.all_gather(filled, "zh", axis=0, tiled=False)
    far = lax.ppermute(near, "core", [(0, 1), (1, 0)])
    gathered = lax.all_to_all(asked, around, 0, 0, tiled=True)
    gathered = touch(gathered)
    gathered = gathered.reshape(parts * slots, -1)
    partial = attend(parts, around, gathered, near, far, text_kv, slots, 192)
    returned = lax.all_to_all(partial, around, 0, 0, tiled=True)
    terms = merge(returned, w_out, groups)
    terms = lax.all_to_all(terms, "head", 0, 0, tiled=True)
    stats = norm(
        terms, hidden, mod_scale.reshape(-1, 128), mod_shift.reshape(-1, 128), w_final
    )
    stats = lax.all_to_all(stats, "head", 0, 0, tiled=True)
    return finish(count, step_row, pos, stats, latent, cached_velocity)


def solution(mesh):
    in_specs = (
        P(SEQ, "head"),
        P(None, SEQ, "head"),
        P(None, SEQ, "head"),
        P(None, None, "head"),
        P(SEQ),
        P(SEQ),
        P(SEQ, "head"),
        P("head", None),
        P("head"),
        P("head"),
        P("head", None),
        P(SEQ, None),
        P(SEQ, None),
        P(),
    )
    out_specs = (P(SEQ, None), P(SEQ, None))
    split = jax.sharding.Mesh(
        mesh.devices.reshape(4, 4, 4, 2, mesh.shape["head"]), SEQ + ("head",)
    )

    return jax.shard_map(
        on_device, mesh=split, in_specs=in_specs, out_specs=out_specs, check_vma=False
    )
```

```python
import functools

import jax
import jax.numpy as jnp
from jax import lax
from jax.experimental import pallas as pl
from jax.experimental.pallas import tpu as pltpu
from jax.sharding import PartitionSpec as P


D = 3072
HD = 128
EPS = 1e-06
LOG2E = 1.4426950408889634
SCALE = HD ** (-0.5)
SEQ = ("zb", "za", "y", "core")
STAT = 8


f32 = jnp.float32
bf16 = jnp.bfloat16
VM = pl.BlockSpec(memory_space=pltpu.VMEM)


def grant(mebibytes):
    return pltpu.CompilerParams(vmem_limit_bytes=mebibytes * 2**20)


def local(*arrays):
    return [pltpu.with_memory_space_constraint(x, pltpu.VMEM) for x in arrays]


def remote(*arrays):
    return [pltpu.with_memory_space_constraint(x, pltpu.HBM) for x in arrays]


def one_hot(pos_ref, count_ref, rows, cols):
    local = pos_ref[...] - lax.axis_index(SEQ) * rows
    slot = lax.broadcasted_iota(jnp.int32, (1, cols), 1)
    local = jnp.where(slot < count_ref[...], local, -1)
    return lax.broadcasted_iota(jnp.int32, (rows, cols), 0) == local


def fill_kernel(count_ref, step_ref, pos_ref, new_ref, cache_ref, out_ref, row_ref):
    rows, cols = cache_ref.shape[1], new_ref.shape[1]
    matched = one_hot(pos_ref, count_ref, rows, cols)
    pick = matched.astype(f32)
    keep = jnp.max(pick, axis=1, keepdims=True) < 0.5
    pick = pick.astype(bf16)
    for s in range(2):
        placed = jnp.dot(pick, new_ref[s], preferred_element_type=f32)
        merged = jnp.where(keep, cache_ref[s].astype(f32), placed).astype(bf16)
        out_ref[s] = merged
    row_ref[...] = jnp.broadcast_to(step_ref[...], row_ref.shape)


def fill(count, step_size, pos, new_kv, cache_kv):
    return pl.pallas_call(
        fill_kernel,
        out_shape=(
            pltpu.VMEM(cache_kv.shape, bf16),
            pltpu.VMEM((8, 128), f32),
        ),
        in_specs=[VM] * 5,
        out_specs=(VM, VM),
        compiler_params=grant(8),
    )(count, step_size, *remote(pos, new_kv, cache_kv))


def spread_kernel(own_ref, other_ref, out_ref):
    for d in range(out_ref.shape[0]):
        out_ref[d, 0] = own_ref[...]
        out_ref[d, 1] = other_ref[...]


def spread(own, other, copies):
    return pl.pallas_call(
        spread_kernel,
        out_shape=pltpu.VMEM((copies, 2) + own.shape, bf16),
        in_specs=[VM] * 2,
        out_specs=VM,
        compiler_params=grant(8),
    )(*local(own, other))


def attend_kernel(q_ref, a_ref, b_ref, t_ref, out_ref, *, chunk, around):
    parts = out_ref.shape[0]
    slots = q_ref.shape[0] // parts
    heads = q_ref.shape[1] // HD
    share = t_ref.shape[1] // parts
    own_text = pl.ds(pl.multiple_of(lax.axis_index(around) * share, share), share)
    lane = lax.broadcasted_iota(jnp.int32, (slots, HD), 1)
    slot = lax.broadcasted_iota(jnp.int32, (slots, HD), 0)
    row = lax.broadcasted_iota(jnp.int32, (STAT, HD), 0)
    stats = [jnp.zeros((STAT, HD), f32)] * parts
    for h in range(heads):
        cols = slice(h * HD, (h + 1) * HD)
        eye = lane == slot + slots * (h % 2)
        base = 3 * (h // 2)
        keys, values = [], []
        for ref in (a_ref, b_ref):
            n = ref.shape[0] * ref.shape[1] * ref.shape[3]
            keys.append(ref[:, :, 0, :, cols].reshape(n, HD))
            values.append(ref[:, :, 1, :, cols].reshape(n, HD))
        keys.append(t_ref[0, own_text, cols])
        values.append(t_ref[1, own_text, cols])
        for start in range(0, q_ref.shape[0], chunk):
            q = q_ref[pl.ds(start, chunk), cols]
            scores = [
                lax.dot_general(
                    q, k, (((1,), (1,)), ((), ())), preferred_element_type=f32
                )
                for k in keys
            ]
            top = functools.reduce(
                jnp.maximum, [jnp.max(s, axis=1, keepdims=True) for s in scores]
            )
            weights = [jnp.exp2((s - top) * (SCALE * LOG2E)) for s in scores]
            total = sum(jnp.sum(w, axis=1, keepdims=True) for w in weights)
            mixed = sum(
                jnp.dot(w.astype(bf16), v, preferred_element_type=f32)
                for w, v in zip(weights, values)
            )
            mixed = mixed / total
            level = top * SCALE + jnp.log(total)
            for i in range(chunk // slots):
                d = start // slots + i
                part = slice(i * slots, (i + 1) * slots)
                out_ref[d, h * slots : (h + 1) * slots, :] = mixed[part].astype(bf16)
                line = jnp.sum(
                    jnp.where(eye, level[part], 0.0), axis=0, keepdims=True
                )
                first = line.astype(bf16).astype(f32)
                second = (line - first).astype(bf16).astype(f32)
                third = line - first - second
                for p, piece in enumerate((first, second, third)):
                    stats[d] = jnp.where(row == base + p, stats[d] + piece, stats[d])
    for d in range(parts):
        out_ref[d, heads * slots : heads * slots + STAT, :] = stats[d].astype(bf16)


def attend(parts, around, queries, near, far, text_kv, slots, chunk):
    heads = queries.shape[1] // HD
    return pl.pallas_call(
        functools.partial(attend_kernel, chunk=chunk, around=around),
        out_shape=pltpu.VMEM((parts, heads * slots + STAT, HD), bf16),
        in_specs=[VM] * 4,
        out_specs=VM,
        compiler_params=grant(20),
    )(*local(queries, near, far, text_kv))


def merge_kernel(got_ref, w_ref, out_ref):
    parts, rows, _ = got_ref.shape
    count = w_ref.shape[0] // HD
    slots = (rows - STAT) // count
    stat = got_ref[:, rows - STAT : rows, :].astype(f32)
    shares = []
    for base in range(0, 3 * ((count + 1) // 2), 3):
        level = stat[:, base] + stat[:, base + 1] + stat[:, base + 2]
        share = jnp.exp(level - jnp.max(level, axis=0, keepdims=True))
        share = share / jnp.sum(share, axis=0, keepdims=True)
        pad = jnp.zeros((HD - parts, HD), f32)
        shares.append(jnp.concatenate([share, pad], axis=0).T)
    heads = []
    for h in range(count):
        share = shares[h // 2][slots * (h % 2) : slots * (h % 2 + 1)]
        total = jnp.zeros((slots, HD), f32)
        for s in range(parts):
            block = got_ref[s, h * slots : (h + 1) * slots, :].astype(f32)
            total += block * share[:, s : s + 1]
        heads.append(total.astype(bf16))
    attended = jnp.concatenate(heads, axis=1)
    piece = out_ref.shape[2]
    for k in range(out_ref.shape[0]):
        out_ref[k] = jnp.dot(
            attended, w_ref[:, k * piece : (k + 1) * piece], preferred_element_type=f32
        ).astype(bf16)


def merge(got, w_out, groups):
    slots = (got.shape[1] - STAT) // (w_out.shape[0] // HD)
    return pl.pallas_call(
        merge_kernel,
        out_shape=pltpu.VMEM(
            (groups, slots, w_out.shape[1] // groups), bf16
        ),
        in_specs=[VM, VM],
        out_specs=VM,
        compiler_params=grant(8),
    )(*local(got, w_out))


def flat(ref):
    return jnp.concatenate([ref[i : i + 1, :] for i in range(ref.shape[0])], axis=1)


def norm_kernel(got_ref, hidden_ref, scale_ref, shift_ref, w_ref, out_ref):
    slots, width = hidden_ref.shape
    summed = hidden_ref[...].astype(f32)
    for k in range(got_ref.shape[0]):
        summed += got_ref[k].astype(f32)
    mean = jnp.sum(summed, axis=1, keepdims=True) * (1.0 / width)
    centred = summed - mean
    squares = jnp.sum(centred * centred, axis=1, keepdims=True)
    lifted = 1.0 + flat(scale_ref)
    tail = lax.broadcasted_iota(jnp.int32, (STAT, width), 0)
    tail = jnp.where(tail == 0, lifted, jnp.where(tail == 1, flat(shift_ref), 0.0))
    rows = jnp.concatenate([centred * lifted, tail], axis=0)
    mapped = lax.dot_general(
        rows,
        w_ref[...],
        (((1,), (1,)), ((), ())),
        precision=lax.Precision.HIGHEST,
        preferred_element_type=f32,
    )
    lane = lax.broadcasted_iota(jnp.int32, (slots, 64), 1)
    stat = jnp.where(lane == 0, mean, jnp.where(lane == 1, squares, 0.0))
    stat = jnp.concatenate([stat, jnp.zeros((STAT, 64), f32)], axis=0)
    block = jnp.concatenate([mapped, stat], axis=1)
    for k in range(out_ref.shape[0]):
        out_ref[k] = block


def norm(got, hidden, scale, shift, w_final):
    return pl.pallas_call(
        norm_kernel,
        out_shape=pltpu.VMEM(
            (got.shape[0], hidden.shape[0] + STAT, 2 * w_final.shape[1]), f32
        ),
        in_specs=[VM] * 5,
        out_specs=VM,
        compiler_params=grant(8),
    )(*local(got, hidden, scale, shift, w_final.T))


def finish_kernel(
    count_ref, step_ref, pos_ref, got_ref, latent_ref, old_ref, velocity_ref, next_ref
):
    groups, rows, _ = got_ref.shape
    slots = rows - STAT
    ch = latent_ref.shape[0]
    blocks = [got_ref[k] for k in range(groups)]
    means = [b[0:slots, ch : ch + 1] for b in blocks]
    mean = sum(means) * (1.0 / groups)
    width = D // groups
    var = sum(b[0:slots, ch + 1 : ch + 2] for b in blocks)
    var = (var + width * sum((m - mean) * (m - mean) for m in means)) * (1.0 / D)
    mapped = sum(
        b[0:slots, 0:ch] + (m - mean) * b[slots : slots + 1, 0:ch]
        for b, m in zip(blocks, means)
    )
    base = sum(b[slots + 1 : slots + 2, 0:ch] for b in blocks)
    fresh = mapped * lax.rsqrt(var + EPS) + base
    tokens = latent_ref.shape[1]
    pick = one_hot(pos_ref, count_ref, tokens, slots).astype(f32)
    keep = lax.dot_general(
        jnp.ones((8, slots), f32),
        pick,
        (((1,), (1,)), ((), ())),
        preferred_element_type=f32,
    )[0:1]
    chosen = lax.dot_general(
        fresh,
        pick,
        (((0,), (1,)), ((), ())),
        precision=lax.Precision.HIGHEST,
        preferred_element_type=f32,
    )
    velocity = jnp.where(keep < 0.5, old_ref[...], chosen)
    velocity_ref[...] = velocity
    next_ref[...] = latent_ref[...] + step_ref[0:1, :] * velocity


def finish(count, step_size, pos, got, latent, cached_velocity):
    velocity, following = pl.pallas_call(
        finish_kernel,
        out_shape=(
            jax.ShapeDtypeStruct(latent.shape[::-1], f32),
            jax.ShapeDtypeStruct(latent.shape[::-1], f32),
        ),
        in_specs=[VM] * 6,
        out_specs=(VM, VM),
        compiler_params=grant(8),
    )(count, *local(step_size), pos, *local(got, latent.T, cached_velocity.T))
    return velocity.T, following.T


def on_device(
    query,
    new_kv,
    cache_kv,
    text_kv,
    active,
    counts,
    hidden,
    w_out,
    mod_shift,
    mod_scale,
    w_final,
    latent,
    cached_velocity,
    step_size,
):
    groups = lax.axis_size("head")
    parts = lax.axis_size("zb")
    slots = query.shape[0]
    trade = [(0, 1), (1, 0)]

    count = counts.reshape(1, 1)
    pos = active.reshape(1, slots)
    filled, step_row = fill(count, step_size.reshape(1, 1), pos, new_kv, cache_kv)
    pair = spread(filled, lax.ppermute(filled, "za", trade), lax.axis_size("y"))
    near = lax.all_to_all(pair, "y", 0, 0, tiled=True)
    gathered = lax.all_gather(query, "zb", axis=0, tiled=True)
    far = lax.ppermute(near, "core", trade)
    partial = attend(parts, "zb", gathered, near, far, text_kv, slots, 192)
    returned = lax.all_to_all(partial, "zb", 0, 0, tiled=True)
    terms = merge(returned, w_out, groups)
    terms = lax.all_to_all(terms, "head", 0, 0, tiled=True)
    stats = norm(
        terms, hidden, mod_scale.reshape(-1, 128), mod_shift.reshape(-1, 128), w_final
    )
    stats = lax.all_to_all(stats, "head", 0, 0, tiled=True)
    return finish(count, step_row, pos, stats, latent, cached_velocity)


def solution(mesh):
    in_specs = (
        P(SEQ, "head"),
        P(None, SEQ, "head"),
        P(None, SEQ, "head"),
        P(None, None, "head"),
        P(SEQ),
        P(SEQ),
        P(SEQ, "head"),
        P("head", None),
        P("head"),
        P("head"),
        P("head", None),
        P(SEQ, None),
        P(SEQ, None),
        P(),
    )
    out_specs = (P(SEQ, None), P(SEQ, None))
    split = jax.sharding.Mesh(
        mesh.devices.reshape(8, 2, 4, 2, mesh.shape["head"]), SEQ + ("head",)
    )

    return jax.shard_map(
        on_device, mesh=split, in_specs=in_specs, out_specs=out_specs, check_vma=False
    )
```

```python
import functools

import jax
import jax.numpy as jnp
from jax import lax
from jax.experimental import pallas as pl
from jax.experimental.pallas import tpu as pltpu
from jax.sharding import PartitionSpec as P


D = 3072
HD = 128
EPS = 1e-06
LOG2E = 1.4426950408889634
SCALE = HD ** (-0.5)
SEQ = ("zb", "za", "y", "core")
STAT = 8


f32 = jnp.float32
bf16 = jnp.bfloat16
VM = pl.BlockSpec(memory_space=pltpu.VMEM)


def grant(mebibytes):
    return pltpu.CompilerParams(vmem_limit_bytes=mebibytes * 2**20)


def local(*arrays):
    return [pltpu.with_memory_space_constraint(x, pltpu.VMEM) for x in arrays]


def remote(*arrays):
    return [pltpu.with_memory_space_constraint(x, pltpu.HBM) for x in arrays]


def one_hot(pos_ref, count_ref, rows, cols):
    local = pos_ref[...] - lax.axis_index(SEQ) * rows
    slot = lax.broadcasted_iota(jnp.int32, (1, cols), 1)
    local = jnp.where(slot < count_ref[...], local, -1)
    return lax.broadcasted_iota(jnp.int32, (rows, cols), 0) == local


def fill_kernel(
    count_ref, step_ref, pos_ref, q_ref, new_ref, cache_ref, out_ref, asked_ref, row_ref
):
    rows, cols = cache_ref.shape[1], new_ref.shape[1]
    matched = one_hot(pos_ref, count_ref, rows, cols)
    pick = matched.astype(f32)
    keep = jnp.max(pick, axis=1, keepdims=True) < 0.5
    pick = pick.astype(bf16)
    for s in range(2):
        placed = jnp.dot(pick, new_ref[s], preferred_element_type=f32)
        merged = jnp.where(keep, cache_ref[s].astype(f32), placed).astype(bf16)
        out_ref[s] = merged
    for d in range(asked_ref.shape[0]):
        asked_ref[d] = q_ref[...]
    row_ref[...] = jnp.broadcast_to(step_ref[...], row_ref.shape)


def fill(count, step_size, pos, query, new_kv, cache_kv, copies):
    return pl.pallas_call(
        fill_kernel,
        out_shape=(
            pltpu.VMEM(cache_kv.shape, bf16),
            pltpu.VMEM((copies,) + query.shape, bf16),
            pltpu.VMEM((8, 128), f32),
        ),
        in_specs=[VM] * 6,
        out_specs=(VM, VM, VM),
        compiler_params=grant(8),
    )(count, step_size, *remote(pos, query, new_kv, cache_kv))


def attend_kernel(q_ref, *refs, chunk, around):
    *kv_refs, t_ref, out_ref = refs
    parts = out_ref.shape[0]
    slots = q_ref.shape[0] // parts
    heads = q_ref.shape[1] // HD
    share = t_ref.shape[1] // parts
    own_text = pl.ds(pl.multiple_of(lax.axis_index(around) * share, share), share)
    lane = lax.broadcasted_iota(jnp.int32, (slots, HD), 1)
    slot = lax.broadcasted_iota(jnp.int32, (slots, HD), 0)
    row = lax.broadcasted_iota(jnp.int32, (STAT, HD), 0)
    stats = [jnp.zeros((STAT, HD), f32)] * parts
    for h in range(heads):
        cols = slice(h * HD, (h + 1) * HD)
        eye = lane == slot + slots * (h % 2)
        base = 3 * (h // 2)
        keys, values = [], []
        for ref in kv_refs:
            n = ref.shape[0] * ref.shape[2]
            keys.append(ref[:, 0, :, cols].reshape(n, HD))
            values.append(ref[:, 1, :, cols].reshape(n, HD))
        keys.append(t_ref[0, own_text, cols])
        values.append(t_ref[1, own_text, cols])
        for start in range(0, q_ref.shape[0], chunk):
            q = q_ref[pl.ds(start, chunk), cols]
            scores = [
                lax.dot_general(
                    q, k, (((1,), (1,)), ((), ())), preferred_element_type=f32
                )
                for k in keys
            ]
            top = functools.reduce(
                jnp.maximum, [jnp.max(s, axis=1, keepdims=True) for s in scores]
            )
            weights = [jnp.exp2((s - top) * (SCALE * LOG2E)) for s in scores]
            total = sum(jnp.sum(w, axis=1, keepdims=True) for w in weights)
            mixed = sum(
                jnp.dot(w.astype(bf16), v, preferred_element_type=f32)
                for w, v in zip(weights, values)
            )
            mixed = mixed / total
            level = top * SCALE + jnp.log(total)
            for i in range(chunk // slots):
                d = start // slots + i
                part = slice(i * slots, (i + 1) * slots)
                out_ref[d, h * slots : (h + 1) * slots, :] = mixed[part].astype(bf16)
                line = jnp.sum(
                    jnp.where(eye, level[part], 0.0), axis=0, keepdims=True
                )
                first = line.astype(bf16).astype(f32)
                second = (line - first).astype(bf16).astype(f32)
                third = line - first - second
                for p, piece in enumerate((first, second, third)):
                    stats[d] = jnp.where(row == base + p, stats[d] + piece, stats[d])
    for d in range(parts):
        out_ref[d, heads * slots : heads * slots + STAT, :] = stats[d].astype(bf16)


def attend(parts, around, queries, blocks, text_kv, slots, chunk):
    heads = queries.shape[1] // HD
    return pl.pallas_call(
        functools.partial(attend_kernel, chunk=chunk, around=around),
        out_shape=pltpu.VMEM((parts, heads * slots + STAT, HD), bf16),
        in_specs=[VM] * (len(blocks) + 2),
        out_specs=VM,
        compiler_params=grant(20),
    )(*local(queries, *blocks, text_kv))


def merge_kernel(got_ref, w_ref, out_ref):
    parts, rows, _ = got_ref.shape
    count = w_ref.shape[0] // HD
    slots = (rows - STAT) // count
    stat = got_ref[:, rows - STAT : rows, :].astype(f32)
    shares = []
    for base in range(0, 3 * ((count + 1) // 2), 3):
        level = stat[:, base] + stat[:, base + 1] + stat[:, base + 2]
        share = jnp.exp(level - jnp.max(level, axis=0, keepdims=True))
        share = share / jnp.sum(share, axis=0, keepdims=True)
        pad = jnp.zeros((HD - parts, HD), f32)
        shares.append(jnp.concatenate([share, pad], axis=0).T)
    heads = []
    for h in range(count):
        share = shares[h // 2][slots * (h % 2) : slots * (h % 2 + 1)]
        total = jnp.zeros((slots, HD), f32)
        for s in range(parts):
            block = got_ref[s, h * slots : (h + 1) * slots, :].astype(f32)
            total += block * share[:, s : s + 1]
        heads.append(total.astype(bf16))
    attended = jnp.concatenate(heads, axis=1)
    piece = out_ref.shape[2]
    for k in range(out_ref.shape[0]):
        out_ref[k] = jnp.dot(
            attended, w_ref[:, k * piece : (k + 1) * piece], preferred_element_type=f32
        ).astype(bf16)


def merge(got, w_out, groups):
    slots = (got.shape[1] - STAT) // (w_out.shape[0] // HD)
    return pl.pallas_call(
        merge_kernel,
        out_shape=pltpu.VMEM(
            (groups, slots, w_out.shape[1] // groups), bf16
        ),
        in_specs=[VM, VM],
        out_specs=VM,
        compiler_params=grant(8),
    )(*local(got, w_out))


def flat(ref):
    return jnp.concatenate([ref[i : i + 1, :] for i in range(ref.shape[0])], axis=1)


def norm_kernel(got_ref, hidden_ref, scale_ref, shift_ref, w_ref, out_ref):
    slots, width = hidden_ref.shape
    summed = hidden_ref[...].astype(f32)
    for k in range(got_ref.shape[0]):
        summed += got_ref[k].astype(f32)
    mean = jnp.sum(summed, axis=1, keepdims=True) * (1.0 / width)
    centred = summed - mean
    squares = jnp.sum(centred * centred, axis=1, keepdims=True)
    lifted = 1.0 + flat(scale_ref)
    tail = lax.broadcasted_iota(jnp.int32, (STAT, width), 0)
    tail = jnp.where(tail == 0, lifted, jnp.where(tail == 1, flat(shift_ref), 0.0))
    rows = jnp.concatenate([centred * lifted, tail], axis=0)
    mapped = lax.dot_general(
        rows,
        w_ref[...],
        (((1,), (1,)), ((), ())),
        precision=lax.Precision.HIGHEST,
        preferred_element_type=f32,
    )
    lane = lax.broadcasted_iota(jnp.int32, (slots, 64), 1)
    stat = jnp.where(lane == 0, mean, jnp.where(lane == 1, squares, 0.0))
    stat = jnp.concatenate([stat, jnp.zeros((STAT, 64), f32)], axis=0)
    block = jnp.concatenate([mapped, stat], axis=1)
    for k in range(out_ref.shape[0]):
        out_ref[k] = block


def norm(got, hidden, scale, shift, w_final):
    return pl.pallas_call(
        norm_kernel,
        out_shape=pltpu.VMEM(
            (got.shape[0], hidden.shape[0] + STAT, 2 * w_final.shape[1]), f32
        ),
        in_specs=[VM] * 5,
        out_specs=VM,
        compiler_params=grant(8),
    )(*local(got, hidden, scale, shift, w_final.T))


def finish_kernel(
    count_ref, step_ref, pos_ref, got_ref, latent_ref, old_ref, velocity_ref, next_ref
):
    groups, rows, _ = got_ref.shape
    slots = rows - STAT
    ch = latent_ref.shape[0]
    blocks = [got_ref[k] for k in range(groups)]
    means = [b[0:slots, ch : ch + 1] for b in blocks]
    mean = sum(means) * (1.0 / groups)
    width = D // groups
    var = sum(b[0:slots, ch + 1 : ch + 2] for b in blocks)
    var = (var + width * sum((m - mean) * (m - mean) for m in means)) * (1.0 / D)
    mapped = sum(
        b[0:slots, 0:ch] + (m - mean) * b[slots : slots + 1, 0:ch]
        for b, m in zip(blocks, means)
    )
    base = sum(b[slots + 1 : slots + 2, 0:ch] for b in blocks)
    fresh = mapped * lax.rsqrt(var + EPS) + base
    tokens = latent_ref.shape[1]
    pick = one_hot(pos_ref, count_ref, tokens, slots).astype(f32)
    keep = lax.dot_general(
        jnp.ones((8, slots), f32),
        pick,
        (((1,), (1,)), ((), ())),
        preferred_element_type=f32,
    )[0:1]
    chosen = lax.dot_general(
        fresh,
        pick,
        (((0,), (1,)), ((), ())),
        precision=lax.Precision.HIGHEST,
        preferred_element_type=f32,
    )
    velocity = jnp.where(keep < 0.5, old_ref[...], chosen)
    velocity_ref[...] = velocity
    next_ref[...] = latent_ref[...] + step_ref[0:1, :] * velocity


def finish(count, step_size, pos, got, latent, cached_velocity):
    velocity, following = pl.pallas_call(
        finish_kernel,
        out_shape=(
            jax.ShapeDtypeStruct(latent.shape[::-1], f32),
            jax.ShapeDtypeStruct(latent.shape[::-1], f32),
        ),
        in_specs=[VM] * 6,
        out_specs=(VM, VM),
        compiler_params=grant(8),
    )(count, *local(step_size), pos, *local(got, latent.T, cached_velocity.T))
    return velocity.T, following.T


def on_device(
    query,
    new_kv,
    cache_kv,
    text_kv,
    active,
    counts,
    hidden,
    w_out,
    mod_shift,
    mod_scale,
    w_final,
    latent,
    cached_velocity,
    step_size,
):
    groups = lax.axis_size("head")
    parts = lax.axis_size("zb")
    slots = query.shape[0]
    trade = [(0, 1), (1, 0)]

    count = counts.reshape(1, 1)
    pos = active.reshape(1, slots)
    filled, asked, step_row = fill(
        count, step_size.reshape(1, 1), pos, query, new_kv, cache_kv, parts
    )
    other = lax.ppermute(filled, "za", trade)
    gathered = lax.all_to_all(asked, "zb", 0, 0, tiled=True)
    gathered = gathered.reshape(parts * slots, -1)
    own = lax.all_gather(filled, "y", axis=0, tiled=False)
    own_far = lax.ppermute(own, "core", trade)
    other = lax.all_gather(other, "y", axis=0, tiled=False)
    other_far = lax.ppermute(other, "core", trade)
    blocks = (own, own_far, other, other_far)
    partial = attend(parts, "zb", gathered, blocks, text_kv, slots, 192)
    returned = lax.all_to_all(partial, "zb", 0, 0, tiled=True)
    terms = merge(returned, w_out, groups)
    terms = lax.all_to_all(terms, "head", 0, 0, tiled=True)
    stats = norm(
        terms, hidden, mod_scale.reshape(-1, 128), mod_shift.reshape(-1, 128), w_final
    )
    stats = lax.all_to_all(stats, "head", 0, 0, tiled=True)
    return finish(count, step_row, pos, stats, latent, cached_velocity)


def solution(mesh):
    in_specs = (
        P(SEQ, "head"),
        P(None, SEQ, "head"),
        P(None, SEQ, "head"),
        P(None, None, "head"),
        P(SEQ),
        P(SEQ),
        P(SEQ, "head"),
        P("head", None),
        P("head"),
        P("head"),
        P("head", None),
        P(SEQ, None),
        P(SEQ, None),
        P(),
    )
    out_specs = (P(SEQ, None), P(SEQ, None))
    split = jax.sharding.Mesh(
        mesh.devices.reshape(8, 2, 4, 2, mesh.shape["head"]), SEQ + ("head",)
    )

    return jax.shard_map(
        on_device, mesh=split, in_specs=in_specs, out_specs=out_specs, check_vma=False
    )
```

```python
import functools

import jax
import jax.numpy as jnp
from jax import lax
from jax.experimental import pallas as pl
from jax.experimental.pallas import tpu as pltpu
from jax.sharding import PartitionSpec as P


D = 3072
HD = 128
EPS = 1e-06
LOG2E = 1.4426950408889634
SCALE = HD ** (-0.5)
SEQ = ("zh", "zq", "za", "y", "core")
STAT = 8


f32 = jnp.float32
bf16 = jnp.bfloat16
VM = pl.BlockSpec(memory_space=pltpu.VMEM)


def grant(mebibytes):
    return pltpu.CompilerParams(vmem_limit_bytes=mebibytes * 2**20)


def local(*arrays):
    return [pltpu.with_memory_space_constraint(x, pltpu.VMEM) for x in arrays]


def remote(*arrays):
    return [pltpu.with_memory_space_constraint(x, pltpu.HBM) for x in arrays]


def one_hot(pos_ref, count_ref, rows, cols):
    local = pos_ref[...] - lax.axis_index(SEQ) * rows
    slot = lax.broadcasted_iota(jnp.int32, (1, cols), 1)
    local = jnp.where(slot < count_ref[...], local, -1)
    return lax.broadcasted_iota(jnp.int32, (rows, cols), 0) == local


def fill_kernel(count_ref, step_ref, pos_ref, new_ref, cache_ref, out_ref, row_ref):
    rows, cols = cache_ref.shape[1], new_ref.shape[1]
    matched = one_hot(pos_ref, count_ref, rows, cols)
    pick = matched.astype(f32)
    keep = jnp.max(pick, axis=1, keepdims=True) < 0.5
    pick = pick.astype(bf16)
    for s in range(2):
        placed = jnp.dot(pick, new_ref[s], preferred_element_type=f32)
        merged = jnp.where(keep, cache_ref[s].astype(f32), placed).astype(bf16)
        out_ref[s] = merged
    row_ref[...] = jnp.broadcast_to(step_ref[...], row_ref.shape)


def fill(count, step_size, pos, new_kv, cache_kv):
    return pl.pallas_call(
        fill_kernel,
        out_shape=(
            pltpu.VMEM(cache_kv.shape, bf16),
            pltpu.VMEM((8, 128), f32),
        ),
        in_specs=[VM] * 5,
        out_specs=(VM, VM),
        compiler_params=grant(8),
    )(count, step_size, *remote(pos, new_kv, cache_kv))


def spread_kernel(own_ref, other_ref, out_ref):
    for d in range(out_ref.shape[0]):
        out_ref[d, 0] = own_ref[...]
        out_ref[d, 1] = other_ref[...]


def spread(own, other, copies):
    return pl.pallas_call(
        spread_kernel,
        out_shape=pltpu.VMEM((copies, 2) + own.shape, bf16),
        in_specs=[VM] * 2,
        out_specs=VM,
        compiler_params=grant(8),
    )(*local(own, other))


def attend_kernel(q_ref, a_ref, b_ref, t_ref, out_ref, *, chunk, around):
    parts = out_ref.shape[0]
    slots = q_ref.shape[0] // parts
    heads = q_ref.shape[1] // HD
    share = t_ref.shape[1] // parts
    own_text = pl.ds(pl.multiple_of(lax.axis_index(around) * share, share), share)
    lane = lax.broadcasted_iota(jnp.int32, (slots, HD), 1)
    slot = lax.broadcasted_iota(jnp.int32, (slots, HD), 0)
    row = lax.broadcasted_iota(jnp.int32, (STAT, HD), 0)
    stats = [jnp.zeros((STAT, HD), f32)] * parts
    for h in range(heads):
        cols = slice(h * HD, (h + 1) * HD)
        eye = lane == slot + slots * (h % 2)
        base = 3 * (h // 2)
        keys, values = [], []
        for ref in (a_ref, b_ref):
            n = ref.shape[0] * ref.shape[1] * ref.shape[3]
            keys.append(ref[:, :, 0, :, cols].reshape(n, HD))
            values.append(ref[:, :, 1, :, cols].reshape(n, HD))
        keys.append(t_ref[0, own_text, cols])
        values.append(t_ref[1, own_text, cols])
        for start in range(0, q_ref.shape[0], chunk):
            q = q_ref[pl.ds(start, chunk), cols]
            scores = [
                lax.dot_general(
                    q, k, (((1,), (1,)), ((), ())), preferred_element_type=f32
                )
                for k in keys
            ]
            top = functools.reduce(
                jnp.maximum, [jnp.max(s, axis=1, keepdims=True) for s in scores]
            )
            weights = [jnp.exp2((s - top) * (SCALE * LOG2E)) for s in scores]
            total = sum(jnp.sum(w, axis=1, keepdims=True) for w in weights)
            mixed = sum(
                jnp.dot(w.astype(bf16), v, preferred_element_type=f32)
                for w, v in zip(weights, values)
            )
            mixed = mixed / total
            level = top * SCALE + jnp.log(total)
            for i in range(chunk // slots):
                d = start // slots + i
                part = slice(i * slots, (i + 1) * slots)
                out_ref[d, h * slots : (h + 1) * slots, :] = mixed[part].astype(bf16)
                line = jnp.sum(
                    jnp.where(eye, level[part], 0.0), axis=0, keepdims=True
                )
                first = line.astype(bf16).astype(f32)
                second = (line - first).astype(bf16).astype(f32)
                third = line - first - second
                for p, piece in enumerate((first, second, third)):
                    stats[d] = jnp.where(row == base + p, stats[d] + piece, stats[d])
    for d in range(parts):
        out_ref[d, heads * slots : heads * slots + STAT, :] = stats[d].astype(bf16)


def attend(parts, around, queries, near, far, text_kv, slots, chunk):
    heads = queries.shape[1] // HD
    return pl.pallas_call(
        functools.partial(attend_kernel, chunk=chunk, around=around),
        out_shape=pltpu.VMEM((parts, heads * slots + STAT, HD), bf16),
        in_specs=[VM] * 4,
        out_specs=VM,
        compiler_params=grant(20),
    )(*local(queries, near, far, text_kv))


def merge_kernel(got_ref, w_ref, out_ref):
    parts, rows, _ = got_ref.shape
    count = w_ref.shape[0] // HD
    slots = (rows - STAT) // count
    stat = got_ref[:, rows - STAT : rows, :].astype(f32)
    shares = []
    for base in range(0, 3 * ((count + 1) // 2), 3):
        level = stat[:, base] + stat[:, base + 1] + stat[:, base + 2]
        share = jnp.exp(level - jnp.max(level, axis=0, keepdims=True))
        share = share / jnp.sum(share, axis=0, keepdims=True)
        pad = jnp.zeros((HD - parts, HD), f32)
        shares.append(jnp.concatenate([share, pad], axis=0).T)
    heads = []
    for h in range(count):
        share = shares[h // 2][slots * (h % 2) : slots * (h % 2 + 1)]
        total = jnp.zeros((slots, HD), f32)
        for s in range(parts):
            block = got_ref[s, h * slots : (h + 1) * slots, :].astype(f32)
            total += block * share[:, s : s + 1]
        heads.append(total.astype(bf16))
    attended = jnp.concatenate(heads, axis=1)
    piece = out_ref.shape[2]
    for k in range(out_ref.shape[0]):
        out_ref[k] = jnp.dot(
            attended, w_ref[:, k * piece : (k + 1) * piece], preferred_element_type=f32
        ).astype(bf16)


def merge(got, w_out, groups):
    slots = (got.shape[1] - STAT) // (w_out.shape[0] // HD)
    return pl.pallas_call(
        merge_kernel,
        out_shape=pltpu.VMEM(
            (groups, slots, w_out.shape[1] // groups), bf16
        ),
        in_specs=[VM, VM],
        out_specs=VM,
        compiler_params=grant(8),
    )(*local(got, w_out))


def flat(ref):
    return jnp.concatenate([ref[i : i + 1, :] for i in range(ref.shape[0])], axis=1)


def norm_kernel(got_ref, hidden_ref, scale_ref, shift_ref, w_ref, out_ref):
    slots, width = hidden_ref.shape
    summed = hidden_ref[...].astype(f32)
    for k in range(got_ref.shape[0]):
        summed += got_ref[k].astype(f32)
    mean = jnp.sum(summed, axis=1, keepdims=True) * (1.0 / width)
    centred = summed - mean
    squares = jnp.sum(centred * centred, axis=1, keepdims=True)
    lifted = 1.0 + flat(scale_ref)
    tail = lax.broadcasted_iota(jnp.int32, (STAT, width), 0)
    tail = jnp.where(tail == 0, lifted, jnp.where(tail == 1, flat(shift_ref), 0.0))
    rows = jnp.concatenate([centred * lifted, tail], axis=0)
    mapped = lax.dot_general(
        rows,
        w_ref[...],
        (((1,), (1,)), ((), ())),
        precision=lax.Precision.HIGHEST,
        preferred_element_type=f32,
    )
    lane = lax.broadcasted_iota(jnp.int32, (slots, 64), 1)
    stat = jnp.where(lane == 0, mean, jnp.where(lane == 1, squares, 0.0))
    stat = jnp.concatenate([stat, jnp.zeros((STAT, 64), f32)], axis=0)
    block = jnp.concatenate([mapped, stat], axis=1)
    for k in range(out_ref.shape[0]):
        out_ref[k] = block


def norm(got, hidden, scale, shift, w_final):
    return pl.pallas_call(
        norm_kernel,
        out_shape=pltpu.VMEM(
            (got.shape[0], hidden.shape[0] + STAT, 2 * w_final.shape[1]), f32
        ),
        in_specs=[VM] * 5,
        out_specs=VM,
        compiler_params=grant(8),
    )(*local(got, hidden, scale, shift, w_final.T))


def finish_kernel(
    count_ref, step_ref, pos_ref, got_ref, latent_ref, old_ref, velocity_ref, next_ref
):
    groups, rows, _ = got_ref.shape
    slots = rows - STAT
    ch = latent_ref.shape[0]
    blocks = [got_ref[k] for k in range(groups)]
    means = [b[0:slots, ch : ch + 1] for b in blocks]
    mean = sum(means) * (1.0 / groups)
    width = D // groups
    var = sum(b[0:slots, ch + 1 : ch + 2] for b in blocks)
    var = (var + width * sum((m - mean) * (m - mean) for m in means)) * (1.0 / D)
    mapped = sum(
        b[0:slots, 0:ch] + (m - mean) * b[slots : slots + 1, 0:ch]
        for b, m in zip(blocks, means)
    )
    base = sum(b[slots + 1 : slots + 2, 0:ch] for b in blocks)
    fresh = mapped * lax.rsqrt(var + EPS) + base
    tokens = latent_ref.shape[1]
    pick = one_hot(pos_ref, count_ref, tokens, slots).astype(f32)
    keep = lax.dot_general(
        jnp.ones((8, slots), f32),
        pick,
        (((1,), (1,)), ((), ())),
        preferred_element_type=f32,
    )[0:1]
    chosen = lax.dot_general(
        fresh,
        pick,
        (((0,), (1,)), ((), ())),
        precision=lax.Precision.HIGHEST,
        preferred_element_type=f32,
    )
    velocity = jnp.where(keep < 0.5, old_ref[...], chosen)
    velocity_ref[...] = velocity
    next_ref[...] = latent_ref[...] + step_ref[0:1, :] * velocity


def finish(count, step_size, pos, got, latent, cached_velocity):
    velocity, following = pl.pallas_call(
        finish_kernel,
        out_shape=(
            jax.ShapeDtypeStruct(latent.shape[::-1], f32),
            jax.ShapeDtypeStruct(latent.shape[::-1], f32),
        ),
        in_specs=[VM] * 6,
        out_specs=(VM, VM),
        compiler_params=grant(8),
    )(count, *local(step_size), pos, *local(got, latent.T, cached_velocity.T))
    return velocity.T, following.T


def on_device(
    query,
    new_kv,
    cache_kv,
    text_kv,
    active,
    counts,
    hidden,
    w_out,
    mod_shift,
    mod_scale,
    w_final,
    latent,
    cached_velocity,
    step_size,
):
    groups = lax.axis_size("head")
    around = ("zh", "zq")
    parts = lax.axis_size(around)
    slots = query.shape[0]
    trade = [(0, 1), (1, 0)]

    count = counts.reshape(1, 1)
    pos = active.reshape(1, slots)
    filled, step_row = fill(count, step_size.reshape(1, 1), pos, new_kv, cache_kv)
    other = lax.ppermute(filled, "za", trade)
    gathered = lax.all_gather(query, "zq", axis=0, tiled=True)
    pair = spread(filled, other, lax.axis_size("y"))
    near = lax.all_to_all(pair, "y", 0, 0, tiled=True)
    gathered = lax.all_gather(gathered, "zh", axis=0, tiled=True)
    far = lax.ppermute(near, "core", trade)
    partial = attend(parts, around, gathered, near, far, text_kv, slots, 192)
    returned = lax.all_to_all(partial, around, 0, 0, tiled=True)
    terms = merge(returned, w_out, groups)
    terms = lax.all_to_all(terms, "head", 0, 0, tiled=True)
    stats = norm(
        terms, hidden, mod_scale.reshape(-1, 128), mod_shift.reshape(-1, 128), w_final
    )
    stats = lax.all_to_all(stats, "head", 0, 0, tiled=True)
    return finish(count, step_row, pos, stats, latent, cached_velocity)


def solution(mesh):
    in_specs = (
        P(SEQ, "head"),
        P(None, SEQ, "head"),
        P(None, SEQ, "head"),
        P(None, None, "head"),
        P(SEQ),
        P(SEQ),
        P(SEQ, "head"),
        P("head", None),
        P("head"),
        P("head"),
        P("head", None),
        P(SEQ, None),
        P(SEQ, None),
        P(),
    )
    out_specs = (P(SEQ, None), P(SEQ, None))
    split = jax.sharding.Mesh(
        mesh.devices.reshape(4, 2, 2, 4, 2, mesh.shape["head"]), SEQ + ("head",)
    )

    return jax.shard_map(
        on_device, mesh=split, in_specs=in_specs, out_specs=out_specs, check_vma=False
    )
```

```python
import functools

import jax
import jax.numpy as jnp
from jax import lax
from jax.experimental import pallas as pl
from jax.experimental.pallas import tpu as pltpu
from jax.sharding import PartitionSpec as P


D = 3072
HD = 128
EPS = 1e-06
LOG2E = 1.4426950408889634
SCALE = HD ** (-0.5)
SEQ = ("zh", "zq", "za", "y", "core")
STAT = 8


f32 = jnp.float32
bf16 = jnp.bfloat16
VM = pl.BlockSpec(memory_space=pltpu.VMEM)


def grant(mebibytes):
    return pltpu.CompilerParams(vmem_limit_bytes=mebibytes * 2**20)


def local(*arrays):
    return [pltpu.with_memory_space_constraint(x, pltpu.VMEM) for x in arrays]


def remote(*arrays):
    return [pltpu.with_memory_space_constraint(x, pltpu.HBM) for x in arrays]


def one_hot(pos_ref, count_ref, rows, cols):
    local = pos_ref[...] - lax.axis_index(SEQ) * rows
    slot = lax.broadcasted_iota(jnp.int32, (1, cols), 1)
    local = jnp.where(slot < count_ref[...], local, -1)
    return lax.broadcasted_iota(jnp.int32, (rows, cols), 0) == local


def fill_kernel(count_ref, step_ref, pos_ref, new_ref, cache_ref, out_ref, row_ref):
    rows, cols = cache_ref.shape[1], new_ref.shape[1]
    matched = one_hot(pos_ref, count_ref, rows, cols)
    pick = matched.astype(f32)
    keep = jnp.max(pick, axis=1, keepdims=True) < 0.5
    pick = pick.astype(bf16)
    for s in range(2):
        placed = jnp.dot(pick, new_ref[s], preferred_element_type=f32)
        merged = jnp.where(keep, cache_ref[s].astype(f32), placed).astype(bf16)
        out_ref[s] = merged
    row_ref[...] = jnp.broadcast_to(step_ref[...], row_ref.shape)


def fill(count, step_size, pos, new_kv, cache_kv):
    return pl.pallas_call(
        fill_kernel,
        out_shape=(
            pltpu.VMEM(cache_kv.shape, bf16),
            pltpu.VMEM((8, 128), f32),
        ),
        in_specs=[VM] * 5,
        out_specs=(VM, VM),
        compiler_params=grant(8),
    )(count, step_size, *remote(pos, new_kv, cache_kv))


def spread_kernel(own_ref, other_ref, out_ref):
    for d in range(out_ref.shape[0]):
        out_ref[d, 0] = own_ref[...]
        out_ref[d, 1] = other_ref[...]


def spread(own, other, copies):
    return pl.pallas_call(
        spread_kernel,
        out_shape=pltpu.VMEM((copies, 2) + own.shape, bf16),
        in_specs=[VM] * 2,
        out_specs=VM,
        compiler_params=grant(8),
    )(*local(own, other))


def attend_kernel(q_ref, a_ref, b_ref, t_ref, out_ref, *, chunk, around):
    parts = out_ref.shape[0]
    inner = lax.axis_size(around[-1])
    place = [d % inner * (parts // inner) + d // inner for d in range(parts)]
    slots = q_ref.shape[0] // parts
    heads = q_ref.shape[1] // HD
    share = t_ref.shape[1] // parts
    own_text = pl.ds(pl.multiple_of(lax.axis_index(around) * share, share), share)
    lane = lax.broadcasted_iota(jnp.int32, (slots, HD), 1)
    slot = lax.broadcasted_iota(jnp.int32, (slots, HD), 0)
    row = lax.broadcasted_iota(jnp.int32, (STAT, HD), 0)
    stats = [jnp.zeros((STAT, HD), f32)] * parts
    for h in range(heads):
        cols = slice(h * HD, (h + 1) * HD)
        eye = lane == slot + slots * (h % 2)
        base = 3 * (h // 2)
        keys, values = [], []
        for ref in (a_ref, b_ref):
            n = ref.shape[0] * ref.shape[1] * ref.shape[3]
            keys.append(ref[:, :, 0, :, cols].reshape(n, HD))
            values.append(ref[:, :, 1, :, cols].reshape(n, HD))
        keys.append(t_ref[0, own_text, cols])
        values.append(t_ref[1, own_text, cols])
        for start in range(0, q_ref.shape[0], chunk):
            q = q_ref[pl.ds(start, chunk), cols]
            scores = [
                lax.dot_general(
                    q, k, (((1,), (1,)), ((), ())), preferred_element_type=f32
                )
                for k in keys
            ]
            top = functools.reduce(
                jnp.maximum, [jnp.max(s, axis=1, keepdims=True) for s in scores]
            )
            weights = [jnp.exp2((s - top) * (SCALE * LOG2E)) for s in scores]
            total = sum(jnp.sum(w, axis=1, keepdims=True) for w in weights)
            mixed = sum(
                jnp.dot(w.astype(bf16), v, preferred_element_type=f32)
                for w, v in zip(weights, values)
            )
            mixed = mixed / total
            level = top * SCALE + jnp.log(total)
            for i in range(chunk // slots):
                d = start // slots + i
                part = slice(i * slots, (i + 1) * slots)
                out_ref[place[d], h * slots : (h + 1) * slots, :] = mixed[part].astype(
                    bf16
                )
                line = jnp.sum(
                    jnp.where(eye, level[part], 0.0), axis=0, keepdims=True
                )
                first = line.astype(bf16).astype(f32)
                second = (line - first).astype(bf16).astype(f32)
                third = line - first - second
                for p, piece in enumerate((first, second, third)):
                    stats[d] = jnp.where(row == base + p, stats[d] + piece, stats[d])
    for d in range(parts):
        out_ref[place[d], heads * slots : heads * slots + STAT, :] = stats[d].astype(
            bf16
        )


def attend(parts, around, queries, near, far, text_kv, slots, chunk):
    heads = queries.shape[1] // HD
    return pl.pallas_call(
        functools.partial(attend_kernel, chunk=chunk, around=around),
        out_shape=pltpu.VMEM((parts, heads * slots + STAT, HD), bf16),
        in_specs=[VM] * 4,
        out_specs=VM,
        compiler_params=grant(20),
    )(*local(queries, near, far, text_kv))


def blend_kernel(got_ref, out_ref, *, slots):
    dests, rows, _ = out_ref.shape
    parts = got_ref.shape[0]
    count = (rows - STAT) // slots
    row = lax.broadcasted_iota(jnp.int32, (STAT, HD), 0)
    stat = got_ref[:, rows - STAT : rows, :].astype(f32)
    stats = [jnp.zeros((STAT, HD), f32)] * dests
    shares = []
    for base in range(0, 3 * ((count + 1) // 2), 3):
        level = stat[:, base] + stat[:, base + 1] + stat[:, base + 2]
        levels = [level[i : i + dests] for i in range(0, parts, dests)]
        top = functools.reduce(jnp.maximum, levels)
        joint = top + jnp.log(sum(jnp.exp(x - top) for x in levels))
        pad = jnp.zeros((HD - parts, HD), f32)
        share = jnp.concatenate([jnp.exp(x - joint) for x in levels] + [pad], axis=0)
        shares.append(share.T)
        first = joint.astype(bf16).astype(f32)
        second = (joint - first).astype(bf16).astype(f32)
        third = joint - first - second
        for p, piece in enumerate((first, second, third)):
            for d in range(dests):
                stats[d] = jnp.where(row == base + p, piece[d : d + 1], stats[d])
    for d in range(dests):
        for h in range(count):
            share = shares[h // 2][slots * (h % 2) : slots * (h % 2 + 1)]
            total = jnp.zeros((slots, HD), f32)
            for s in range(d, parts, dests):
                block = got_ref[s, h * slots : (h + 1) * slots, :].astype(f32)
                total += block * share[:, s : s + 1]
            out_ref[d, h * slots : (h + 1) * slots, :] = total.astype(bf16)
        out_ref[d, rows - STAT : rows, :] = stats[d].astype(bf16)


def blend(got, dests, slots):
    return pl.pallas_call(
        functools.partial(blend_kernel, slots=slots),
        out_shape=pltpu.VMEM((dests,) + got.shape[1:], bf16),
        in_specs=[VM],
        out_specs=VM,
        compiler_params=grant(8),
    )(*local(got))


def merge_kernel(got_ref, w_ref, out_ref):
    parts, rows, _ = got_ref.shape
    count = w_ref.shape[0] // HD
    slots = (rows - STAT) // count
    stat = got_ref[:, rows - STAT : rows, :].astype(f32)
    shares = []
    for base in range(0, 3 * ((count + 1) // 2), 3):
        level = stat[:, base] + stat[:, base + 1] + stat[:, base + 2]
        share = jnp.exp(level - jnp.max(level, axis=0, keepdims=True))
        share = share / jnp.sum(share, axis=0, keepdims=True)
        pad = jnp.zeros((HD - parts, HD), f32)
        shares.append(jnp.concatenate([share, pad], axis=0).T)
    heads = []
    for h in range(count):
        share = shares[h // 2][slots * (h % 2) : slots * (h % 2 + 1)]
        total = jnp.zeros((slots, HD), f32)
        for s in range(parts):
            block = got_ref[s, h * slots : (h + 1) * slots, :].astype(f32)
            total += block * share[:, s : s + 1]
        heads.append(total.astype(bf16))
    attended = jnp.concatenate(heads, axis=1)
    piece = out_ref.shape[2]
    for k in range(out_ref.shape[0]):
        out_ref[k] = jnp.dot(
            attended, w_ref[:, k * piece : (k + 1) * piece], preferred_element_type=f32
        ).astype(bf16)


def merge(got, w_out, groups):
    slots = (got.shape[1] - STAT) // (w_out.shape[0] // HD)
    return pl.pallas_call(
        merge_kernel,
        out_shape=pltpu.VMEM(
            (groups, slots, w_out.shape[1] // groups), bf16
        ),
        in_specs=[VM, VM],
        out_specs=VM,
        compiler_params=grant(8),
    )(*local(got, w_out))


def flat(ref):
    return jnp.concatenate([ref[i : i + 1, :] for i in range(ref.shape[0])], axis=1)


def norm_kernel(got_ref, hidden_ref, scale_ref, shift_ref, w_ref, out_ref):
    slots, width = hidden_ref.shape
    summed = hidden_ref[...].astype(f32)
    for k in range(got_ref.shape[0]):
        summed += got_ref[k].astype(f32)
    mean = jnp.sum(summed, axis=1, keepdims=True) * (1.0 / width)
    centred = summed - mean
    squares = jnp.sum(centred * centred, axis=1, keepdims=True)
    lifted = 1.0 + flat(scale_ref)
    tail = lax.broadcasted_iota(jnp.int32, (STAT, width), 0)
    tail = jnp.where(tail == 0, lifted, jnp.where(tail == 1, flat(shift_ref), 0.0))
    rows = jnp.concatenate([centred * lifted, tail], axis=0)
    mapped = lax.dot_general(
        rows,
        w_ref[...],
        (((1,), (1,)), ((), ())),
        precision=lax.Precision.HIGHEST,
        preferred_element_type=f32,
    )
    lane = lax.broadcasted_iota(jnp.int32, (slots, 64), 1)
    stat = jnp.where(lane == 0, mean, jnp.where(lane == 1, squares, 0.0))
    stat = jnp.concatenate([stat, jnp.zeros((STAT, 64), f32)], axis=0)
    block = jnp.concatenate([mapped, stat], axis=1)
    for k in range(out_ref.shape[0]):
        out_ref[k] = block


def norm(got, hidden, scale, shift, w_final):
    return pl.pallas_call(
        norm_kernel,
        out_shape=pltpu.VMEM(
            (got.shape[0], hidden.shape[0] + STAT, 2 * w_final.shape[1]), f32
        ),
        in_specs=[VM] * 5,
        out_specs=VM,
        compiler_params=grant(8),
    )(*local(got, hidden, scale, shift, w_final.T))


def finish_kernel(
    count_ref, step_ref, pos_ref, got_ref, latent_ref, old_ref, velocity_ref, next_ref
):
    groups, rows, _ = got_ref.shape
    slots = rows - STAT
    ch = latent_ref.shape[0]
    blocks = [got_ref[k] for k in range(groups)]
    means = [b[0:slots, ch : ch + 1] for b in blocks]
    mean = sum(means) * (1.0 / groups)
    width = D // groups
    var = sum(b[0:slots, ch + 1 : ch + 2] for b in blocks)
    var = (var + width * sum((m - mean) * (m - mean) for m in means)) * (1.0 / D)
    mapped = sum(
        b[0:slots, 0:ch] + (m - mean) * b[slots : slots + 1, 0:ch]
        for b, m in zip(blocks, means)
    )
    base = sum(b[slots + 1 : slots + 2, 0:ch] for b in blocks)
    fresh = mapped * lax.rsqrt(var + EPS) + base
    tokens = latent_ref.shape[1]
    pick = one_hot(pos_ref, count_ref, tokens, slots).astype(f32)
    keep = lax.dot_general(
        jnp.ones((8, slots), f32),
        pick,
        (((1,), (1,)), ((), ())),
        preferred_element_type=f32,
    )[0:1]
    chosen = lax.dot_general(
        fresh,
        pick,
        (((0,), (1,)), ((), ())),
        precision=lax.Precision.HIGHEST,
        preferred_element_type=f32,
    )
    velocity = jnp.where(keep < 0.5, old_ref[...], chosen)
    velocity_ref[...] = velocity
    next_ref[...] = latent_ref[...] + step_ref[0:1, :] * velocity


def finish(count, step_size, pos, got, latent, cached_velocity):
    velocity, following = pl.pallas_call(
        finish_kernel,
        out_shape=(
            jax.ShapeDtypeStruct(latent.shape[::-1], f32),
            jax.ShapeDtypeStruct(latent.shape[::-1], f32),
        ),
        in_specs=[VM] * 6,
        out_specs=(VM, VM),
        compiler_params=grant(8),
    )(count, *local(step_size), pos, *local(got, latent.T, cached_velocity.T))
    return velocity.T, following.T


def on_device(
    query,
    new_kv,
    cache_kv,
    text_kv,
    active,
    counts,
    hidden,
    w_out,
    mod_shift,
    mod_scale,
    w_final,
    latent,
    cached_velocity,
    step_size,
):
    groups = lax.axis_size("head")
    around = ("zh", "zq")
    parts = lax.axis_size(around)
    slots = query.shape[0]
    trade = [(0, 1), (1, 0)]

    count = counts.reshape(1, 1)
    pos = active.reshape(1, slots)
    filled, step_row = fill(count, step_size.reshape(1, 1), pos, new_kv, cache_kv)
    other = lax.ppermute(filled, "za", trade)
    gathered = lax.all_gather(query, "zq", axis=0, tiled=True)
    pair = spread(filled, other, lax.axis_size("y"))
    near = lax.all_to_all(pair, "y", 0, 0, tiled=True)
    gathered = lax.all_gather(gathered, "zh", axis=0, tiled=True)
    far = lax.ppermute(near, "core", trade)
    partial = attend(parts, around, gathered, near, far, text_kv, slots, 192)
    partial = lax.all_to_all(partial, "zq", 0, 0, tiled=True)
    partial = blend(partial, lax.axis_size("zh"), slots)
    returned = lax.all_to_all(partial, "zh", 0, 0, tiled=True)
    terms = merge(returned, w_out, groups)
    terms = lax.all_to_all(terms, "head", 0, 0, tiled=True)
    stats = norm(
        terms, hidden, mod_scale.reshape(-1, 128), mod_shift.reshape(-1, 128), w_final
    )
    stats = lax.all_to_all(stats, "head", 0, 0, tiled=True)
    return finish(count, step_row, pos, stats, latent, cached_velocity)


def solution(mesh):
    in_specs = (
        P(SEQ, "head"),
        P(None, SEQ, "head"),
        P(None, SEQ, "head"),
        P(None, None, "head"),
        P(SEQ),
        P(SEQ),
        P(SEQ, "head"),
        P("head", None),
        P("head"),
        P("head"),
        P("head", None),
        P(SEQ, None),
        P(SEQ, None),
        P(),
    )
    out_specs = (P(SEQ, None), P(SEQ, None))
    split = jax.sharding.Mesh(
        mesh.devices.reshape(4, 2, 2, 4, 2, mesh.shape["head"]), SEQ + ("head",)
    )

    return jax.shard_map(
        on_device, mesh=split, in_specs=in_specs, out_specs=out_specs, check_vma=False
    )
```

```python
import functools

import jax
import jax.numpy as jnp
from jax import lax
from jax.experimental import pallas as pl
from jax.experimental.pallas import tpu as pltpu
from jax.sharding import PartitionSpec as P


D = 3072
HD = 128
EPS = 1e-06
LOG2E = 1.4426950408889634
SCALE = HD ** (-0.5)
SEQ = ("zh", "zq", "za", "y", "core")
STAT = 8


f32 = jnp.float32
bf16 = jnp.bfloat16
VM = pl.BlockSpec(memory_space=pltpu.VMEM)


def grant(mebibytes):
    return pltpu.CompilerParams(vmem_limit_bytes=mebibytes * 2**20)


def local(*arrays):
    return [pltpu.with_memory_space_constraint(x, pltpu.VMEM) for x in arrays]


def remote(*arrays):
    return [pltpu.with_memory_space_constraint(x, pltpu.HBM) for x in arrays]


def one_hot(pos_ref, count_ref, rows, cols):
    local = pos_ref[...] - lax.axis_index(SEQ) * rows
    slot = lax.broadcasted_iota(jnp.int32, (1, cols), 1)
    local = jnp.where(slot < count_ref[...], local, -1)
    return lax.broadcasted_iota(jnp.int32, (rows, cols), 0) == local


def fill_kernel(count_ref, step_ref, pos_ref, new_ref, cache_ref, out_ref, row_ref):
    rows, cols = cache_ref.shape[1], new_ref.shape[1]
    matched = one_hot(pos_ref, count_ref, rows, cols)
    pick = matched.astype(f32)
    keep = jnp.max(pick, axis=1, keepdims=True) < 0.5
    pick = pick.astype(bf16)
    for s in range(2):
        placed = jnp.dot(pick, new_ref[s], preferred_element_type=f32)
        merged = jnp.where(keep, cache_ref[s].astype(f32), placed).astype(bf16)
        out_ref[s] = merged
    row_ref[...] = jnp.broadcast_to(step_ref[...], row_ref.shape)


def fill(count, step_size, pos, new_kv, cache_kv):
    return pl.pallas_call(
        fill_kernel,
        out_shape=(
            pltpu.VMEM(cache_kv.shape, bf16),
            pltpu.VMEM((8, 128), f32),
        ),
        in_specs=[VM] * 5,
        out_specs=(VM, VM),
        compiler_params=grant(8),
    )(count, step_size, *remote(pos, new_kv, cache_kv))


def spread_kernel(own_ref, other_ref, out_ref):
    for d in range(out_ref.shape[0]):
        out_ref[d, 0] = own_ref[...]
        out_ref[d, 1] = other_ref[...]


def spread(own, other, copies):
    return pl.pallas_call(
        spread_kernel,
        out_shape=pltpu.VMEM((copies, 2) + own.shape, bf16),
        in_specs=[VM] * 2,
        out_specs=VM,
        compiler_params=grant(8),
    )(*local(own, other))


def attend_part(q, keys, values):
    scores = [
        lax.dot_general(q, k, (((1,), (1,)), ((), ())), preferred_element_type=f32)
        for k in keys
    ]
    top = functools.reduce(
        jnp.maximum, [jnp.max(s, axis=1, keepdims=True) for s in scores]
    )
    weights = [jnp.exp2((s - top) * (SCALE * LOG2E)) for s in scores]
    total = sum(jnp.sum(w, axis=1, keepdims=True) for w in weights)
    mixed = sum(
        jnp.dot(w.astype(bf16), v, preferred_element_type=f32)
        for w, v in zip(weights, values)
    )
    return top, total, mixed


def flat_keys(ref, side, cols):
    n = ref.shape[0] * ref.shape[1] * ref.shape[3]
    return ref[:, :, side, :, cols].reshape(n, HD)


def near_kernel(q_ref, a_ref, t_ref, mixed_ref, stat_ref, *, chunk, parts, around):
    share = t_ref.shape[1] // parts
    own_text = pl.ds(pl.multiple_of(lax.axis_index(around) * share, share), share)
    lane = lax.broadcasted_iota(jnp.int32, (chunk, HD), 1)
    heads = q_ref.shape[1] // HD
    for start in range(0, q_ref.shape[0], chunk):
        rows = pl.ds(start, chunk)
        stat = jnp.zeros((chunk, HD), f32)
        for h in range(heads):
            cols = slice(h * HD, (h + 1) * HD)
            top, total, mixed = attend_part(
                q_ref[rows, cols],
                [flat_keys(a_ref, 0, cols), t_ref[0, own_text, cols]],
                [flat_keys(a_ref, 1, cols), t_ref[1, own_text, cols]],
            )
            mixed_ref[rows, cols] = mixed
            stat = jnp.where(lane == h, top, jnp.where(lane == heads + h, total, stat))
        stat_ref[rows, :] = stat


def attend_near(parts, around, queries, near, text_kv, chunk):
    return pl.pallas_call(
        functools.partial(near_kernel, chunk=chunk, parts=parts, around=around),
        out_shape=(
            pltpu.VMEM(queries.shape, f32),
            pltpu.VMEM((queries.shape[0], HD), f32),
        ),
        in_specs=[VM] * 3,
        out_specs=(VM, VM),
        compiler_params=grant(20),
    )(*local(queries, near, text_kv))


def far_kernel(q_ref, b_ref, mixed_ref, stat_ref, out_ref, *, chunk):
    parts = out_ref.shape[0]
    slots = q_ref.shape[0] // parts
    heads = q_ref.shape[1] // HD
    lane = lax.broadcasted_iota(jnp.int32, (slots, HD), 1)
    slot = lax.broadcasted_iota(jnp.int32, (slots, HD), 0)
    row = lax.broadcasted_iota(jnp.int32, (STAT, HD), 0)
    stats = [jnp.zeros((STAT, HD), f32)] * parts
    for h in range(heads):
        cols = slice(h * HD, (h + 1) * HD)
        eye = lane == slot + slots * (h % 2)
        base = 3 * (h // 2)
        for start in range(0, q_ref.shape[0], chunk):
            rows = pl.ds(start, chunk)
            far_top, far_total, mixed = attend_part(
                q_ref[rows, cols],
                [flat_keys(b_ref, 0, cols)],
                [flat_keys(b_ref, 1, cols)],
            )
            near_top = stat_ref[rows, h : h + 1]
            near_total = stat_ref[rows, heads + h : heads + h + 1]
            top = jnp.maximum(near_top, far_top)
            near_scale = jnp.exp2((near_top - top) * (SCALE * LOG2E))
            far_scale = jnp.exp2((far_top - top) * (SCALE * LOG2E))
            total = near_total * near_scale + far_total * far_scale
            mixed = mixed_ref[rows, cols] * (near_scale / total) + mixed * (
                far_scale / total
            )
            level = top * SCALE + jnp.log(total)
            for i in range(chunk // slots):
                d = start // slots + i
                part = slice(i * slots, (i + 1) * slots)
                out_ref[d, h * slots : (h + 1) * slots, :] = mixed[part].astype(bf16)
                line = jnp.sum(
                    jnp.where(eye, level[part], 0.0), axis=0, keepdims=True
                )
                first = line.astype(bf16).astype(f32)
                second = (line - first).astype(bf16).astype(f32)
                third = line - first - second
                for p, piece in enumerate((first, second, third)):
                    stats[d] = jnp.where(row == base + p, stats[d] + piece, stats[d])
    for d in range(parts):
        out_ref[d, heads * slots : heads * slots + STAT, :] = stats[d].astype(bf16)


def attend_far(parts, queries, far, mixed, stat, slots, chunk):
    heads = queries.shape[1] // HD
    return pl.pallas_call(
        functools.partial(far_kernel, chunk=chunk),
        out_shape=pltpu.VMEM((parts, heads * slots + STAT, HD), bf16),
        in_specs=[VM] * 4,
        out_specs=VM,
        compiler_params=grant(20),
    )(*local(queries, far, mixed, stat))


def merge_kernel(got_ref, w_ref, out_ref):
    parts, rows, _ = got_ref.shape
    count = w_ref.shape[0] // HD
    slots = (rows - STAT) // count
    stat = got_ref[:, rows - STAT : rows, :].astype(f32)
    shares = []
    for base in range(0, 3 * ((count + 1) // 2), 3):
        level = stat[:, base] + stat[:, base + 1] + stat[:, base + 2]
        share = jnp.exp(level - jnp.max(level, axis=0, keepdims=True))
        share = share / jnp.sum(share, axis=0, keepdims=True)
        pad = jnp.zeros((HD - parts, HD), f32)
        shares.append(jnp.concatenate([share, pad], axis=0).T)
    heads = []
    for h in range(count):
        share = shares[h // 2][slots * (h % 2) : slots * (h % 2 + 1)]
        total = jnp.zeros((slots, HD), f32)
        for s in range(parts):
            block = got_ref[s, h * slots : (h + 1) * slots, :].astype(f32)
            total += block * share[:, s : s + 1]
        heads.append(total.astype(bf16))
    attended = jnp.concatenate(heads, axis=1)
    piece = out_ref.shape[2]
    for k in range(out_ref.shape[0]):
        out_ref[k] = jnp.dot(
            attended, w_ref[:, k * piece : (k + 1) * piece], preferred_element_type=f32
        ).astype(bf16)


def merge(got, w_out, groups):
    slots = (got.shape[1] - STAT) // (w_out.shape[0] // HD)
    return pl.pallas_call(
        merge_kernel,
        out_shape=pltpu.VMEM(
            (groups, slots, w_out.shape[1] // groups), bf16
        ),
        in_specs=[VM, VM],
        out_specs=VM,
        compiler_params=grant(8),
    )(*local(got, w_out))


def flat(ref):
    return jnp.concatenate([ref[i : i + 1, :] for i in range(ref.shape[0])], axis=1)


def norm_kernel(got_ref, hidden_ref, scale_ref, shift_ref, w_ref, out_ref):
    slots, width = hidden_ref.shape
    summed = hidden_ref[...].astype(f32)
    for k in range(got_ref.shape[0]):
        summed += got_ref[k].astype(f32)
    mean = jnp.sum(summed, axis=1, keepdims=True) * (1.0 / width)
    centred = summed - mean
    squares = jnp.sum(centred * centred, axis=1, keepdims=True)
    lifted = 1.0 + flat(scale_ref)
    tail = lax.broadcasted_iota(jnp.int32, (STAT, width), 0)
    tail = jnp.where(tail == 0, lifted, jnp.where(tail == 1, flat(shift_ref), 0.0))
    rows = jnp.concatenate([centred * lifted, tail], axis=0)
    mapped = lax.dot_general(
        rows,
        w_ref[...],
        (((1,), (1,)), ((), ())),
        precision=lax.Precision.HIGHEST,
        preferred_element_type=f32,
    )
    lane = lax.broadcasted_iota(jnp.int32, (slots, 64), 1)
    stat = jnp.where(lane == 0, mean, jnp.where(lane == 1, squares, 0.0))
    stat = jnp.concatenate([stat, jnp.zeros((STAT, 64), f32)], axis=0)
    block = jnp.concatenate([mapped, stat], axis=1)
    for k in range(out_ref.shape[0]):
        out_ref[k] = block


def norm(got, hidden, scale, shift, w_final):
    return pl.pallas_call(
        norm_kernel,
        out_shape=pltpu.VMEM(
            (got.shape[0], hidden.shape[0] + STAT, 2 * w_final.shape[1]), f32
        ),
        in_specs=[VM] * 5,
        out_specs=VM,
        compiler_params=grant(8),
    )(*local(got, hidden, scale, shift, w_final.T))


def finish_kernel(
    count_ref, step_ref, pos_ref, got_ref, latent_ref, old_ref, velocity_ref, next_ref
):
    groups, rows, _ = got_ref.shape
    slots = rows - STAT
    ch = latent_ref.shape[0]
    blocks = [got_ref[k] for k in range(groups)]
    means = [b[0:slots, ch : ch + 1] for b in blocks]
    mean = sum(means) * (1.0 / groups)
    width = D // groups
    var = sum(b[0:slots, ch + 1 : ch + 2] for b in blocks)
    var = (var + width * sum((m - mean) * (m - mean) for m in means)) * (1.0 / D)
    mapped = sum(
        b[0:slots, 0:ch] + (m - mean) * b[slots : slots + 1, 0:ch]
        for b, m in zip(blocks, means)
    )
    base = sum(b[slots + 1 : slots + 2, 0:ch] for b in blocks)
    fresh = mapped * lax.rsqrt(var + EPS) + base
    tokens = latent_ref.shape[1]
    pick = one_hot(pos_ref, count_ref, tokens, slots).astype(f32)
    keep = lax.dot_general(
        jnp.ones((8, slots), f32),
        pick,
        (((1,), (1,)), ((), ())),
        preferred_element_type=f32,
    )[0:1]
    chosen = lax.dot_general(
        fresh,
        pick,
        (((0,), (1,)), ((), ())),
        precision=lax.Precision.HIGHEST,
        preferred_element_type=f32,
    )
    velocity = jnp.where(keep < 0.5, old_ref[...], chosen)
    velocity_ref[...] = velocity
    next_ref[...] = latent_ref[...] + step_ref[0:1, :] * velocity


def finish(count, step_size, pos, got, latent, cached_velocity):
    velocity, following = pl.pallas_call(
        finish_kernel,
        out_shape=(
            jax.ShapeDtypeStruct(latent.shape[::-1], f32),
            jax.ShapeDtypeStruct(latent.shape[::-1], f32),
        ),
        in_specs=[VM] * 6,
        out_specs=(VM, VM),
        compiler_params=grant(8),
    )(count, *local(step_size), pos, *local(got, latent.T, cached_velocity.T))
    return velocity.T, following.T


def on_device(
    query,
    new_kv,
    cache_kv,
    text_kv,
    active,
    counts,
    hidden,
    w_out,
    mod_shift,
    mod_scale,
    w_final,
    latent,
    cached_velocity,
    step_size,
):
    groups = lax.axis_size("head")
    around = ("zh", "zq")
    parts = lax.axis_size(around)
    slots = query.shape[0]
    trade = [(0, 1), (1, 0)]

    count = counts.reshape(1, 1)
    pos = active.reshape(1, slots)
    filled, step_row = fill(count, step_size.reshape(1, 1), pos, new_kv, cache_kv)
    other = lax.ppermute(filled, "za", trade)
    gathered = lax.all_gather(query, "zq", axis=0, tiled=True)
    pair = spread(filled, other, lax.axis_size("y"))
    near = lax.all_to_all(pair, "y", 0, 0, tiled=True)
    gathered = lax.all_gather(gathered, "zh", axis=0, tiled=True)
    far = lax.ppermute(near, "core", trade)
    mixed, stat = attend_near(parts, around, gathered, near, text_kv, 192)
    partial = attend_far(parts, gathered, far, mixed, stat, slots, 192)
    returned = lax.all_to_all(partial, around, 0, 0, tiled=True)
    terms = merge(returned, w_out, groups)
    terms = lax.all_to_all(terms, "head", 0, 0, tiled=True)
    stats = norm(
        terms, hidden, mod_scale.reshape(-1, 128), mod_shift.reshape(-1, 128), w_final
    )
    stats = lax.all_to_all(stats, "head", 0, 0, tiled=True)
    return finish(count, step_row, pos, stats, latent, cached_velocity)


def solution(mesh):
    in_specs = (
        P(SEQ, "head"),
        P(None, SEQ, "head"),
        P(None, SEQ, "head"),
        P(None, None, "head"),
        P(SEQ),
        P(SEQ),
        P(SEQ, "head"),
        P("head", None),
        P("head"),
        P("head"),
        P("head", None),
        P(SEQ, None),
        P(SEQ, None),
        P(),
    )
    out_specs = (P(SEQ, None), P(SEQ, None))
    split = jax.sharding.Mesh(
        mesh.devices.reshape(4, 2, 2, 4, 2, mesh.shape["head"]), SEQ + ("head",)
    )

    return jax.shard_map(
        on_device, mesh=split, in_specs=in_specs, out_specs=out_specs, check_vma=False
    )
```

```python
import functools

import jax
import jax.numpy as jnp
from jax import lax
from jax.experimental import pallas as pl
from jax.experimental.pallas import tpu as pltpu
from jax.sharding import PartitionSpec as P


D = 3072
HD = 128
EPS = 1e-06
LOG2E = 1.4426950408889634
SCALE = HD ** (-0.5)
SEQ = ("zh", "zq", "za", "y", "core")
STAT = 8


f32 = jnp.float32
bf16 = jnp.bfloat16
VM = pl.BlockSpec(memory_space=pltpu.VMEM)


def grant(mebibytes):
    return pltpu.CompilerParams(vmem_limit_bytes=mebibytes * 2**20)


def local(*arrays):
    return [pltpu.with_memory_space_constraint(x, pltpu.VMEM) for x in arrays]


def remote(*arrays):
    return [pltpu.with_memory_space_constraint(x, pltpu.HBM) for x in arrays]


def one_hot(pos_ref, count_ref, rows, cols):
    local = pos_ref[...] - lax.axis_index(SEQ) * rows
    slot = lax.broadcasted_iota(jnp.int32, (1, cols), 1)
    local = jnp.where(slot < count_ref[...], local, -1)
    return lax.broadcasted_iota(jnp.int32, (rows, cols), 0) == local


def fill_kernel(count_ref, step_ref, pos_ref, new_ref, cache_ref, out_ref, row_ref):
    rows, cols = cache_ref.shape[1], new_ref.shape[1]
    matched = one_hot(pos_ref, count_ref, rows, cols)
    pick = matched.astype(f32)
    keep = jnp.max(pick, axis=1, keepdims=True) < 0.5
    pick = pick.astype(bf16)
    for s in range(2):
        placed = jnp.dot(pick, new_ref[s], preferred_element_type=f32)
        merged = jnp.where(keep, cache_ref[s].astype(f32), placed).astype(bf16)
        out_ref[s] = merged
    row_ref[...] = jnp.broadcast_to(step_ref[...], row_ref.shape)


def fill(count, step_size, pos, new_kv, cache_kv):
    return pl.pallas_call(
        fill_kernel,
        out_shape=(
            pltpu.VMEM(cache_kv.shape, bf16),
            pltpu.VMEM((8, 128), f32),
        ),
        in_specs=[VM] * 5,
        out_specs=(VM, VM),
        compiler_params=grant(8),
    )(count, step_size, *remote(pos, new_kv, cache_kv))


def spread_kernel(own_ref, other_ref, out_ref):
    for d in range(out_ref.shape[0]):
        out_ref[d, 0] = own_ref[...]
        out_ref[d, 1] = other_ref[...]


def spread(own, other, copies):
    return pl.pallas_call(
        spread_kernel,
        out_shape=pltpu.VMEM((copies, 2) + own.shape, bf16),
        in_specs=[VM] * 2,
        out_specs=VM,
        compiler_params=grant(8),
    )(*local(own, other))


def attend_part(q, keys, values):
    scores = [
        lax.dot_general(q, k, (((1,), (1,)), ((), ())), preferred_element_type=f32)
        for k in keys
    ]
    top = functools.reduce(
        jnp.maximum, [jnp.max(s, axis=1, keepdims=True) for s in scores]
    )
    weights = [jnp.exp2((s - top) * (SCALE * LOG2E)) for s in scores]
    total = sum(jnp.sum(w, axis=1, keepdims=True) for w in weights)
    mixed = sum(
        jnp.dot(w.astype(bf16), v, preferred_element_type=f32)
        for w, v in zip(weights, values)
    )
    return top, total, mixed


def flat_keys(ref, side, cols):
    n = ref.shape[0] * ref.shape[1] * ref.shape[3]
    return ref[:, :, side, :, cols].reshape(n, HD)


def near_kernel(q_ref, a_ref, t_ref, mixed_ref, stat_ref, *, chunk, parts, around):
    share = t_ref.shape[1] // parts
    own_text = pl.ds(pl.multiple_of(lax.axis_index(around) * share, share), share)
    heads = q_ref.shape[1] // HD
    for start in range(0, q_ref.shape[0], chunk):
        rows = pl.ds(start, chunk)
        for h in range(heads):
            cols = slice(h * HD, (h + 1) * HD)
            top, total, mixed = attend_part(
                q_ref[rows, cols],
                [flat_keys(a_ref, 0, cols), t_ref[0, own_text, cols]],
                [flat_keys(a_ref, 1, cols), t_ref[1, own_text, cols]],
            )
            mixed_ref[rows, cols] = mixed
            stat_ref[0, rows, cols] = jnp.broadcast_to(top, (chunk, HD))
            stat_ref[1, rows, cols] = jnp.broadcast_to(total, (chunk, HD))


def attend_near(parts, around, queries, near, text_kv, chunk):
    return pl.pallas_call(
        functools.partial(near_kernel, chunk=chunk, parts=parts, around=around),
        out_shape=(
            pltpu.VMEM(queries.shape, f32),
            pltpu.VMEM((2,) + queries.shape, f32),
        ),
        in_specs=[VM] * 3,
        out_specs=(VM, VM),
        compiler_params=grant(20),
    )(*local(queries, near, text_kv))


def far_kernel(q_ref, b_ref, mixed_ref, stat_ref, out_ref, *, chunk):
    parts = out_ref.shape[0]
    slots = q_ref.shape[0] // parts
    heads = q_ref.shape[1] // HD
    lane = lax.broadcasted_iota(jnp.int32, (slots, HD), 1)
    slot = lax.broadcasted_iota(jnp.int32, (slots, HD), 0)
    row = lax.broadcasted_iota(jnp.int32, (STAT, HD), 0)
    stats = [jnp.zeros((STAT, HD), f32)] * parts
    for h in range(heads):
        cols = slice(h * HD, (h + 1) * HD)
        eye = lane == slot + slots * (h % 2)
        base = 3 * (h // 2)
        for start in range(0, q_ref.shape[0], chunk):
            rows = pl.ds(start, chunk)
            far_top, far_total, mixed = attend_part(
                q_ref[rows, cols],
                [flat_keys(b_ref, 0, cols)],
                [flat_keys(b_ref, 1, cols)],
            )
            near_top = stat_ref[0, rows, cols]
            near_total = stat_ref[1, rows, cols]
            far_top = jnp.broadcast_to(far_top, (chunk, HD))
            top = jnp.maximum(near_top, far_top)
            near_scale = jnp.exp2((near_top - top) * (SCALE * LOG2E))
            far_scale = jnp.exp2((far_top - top) * (SCALE * LOG2E))
            total = near_total * near_scale + far_total * far_scale
            mixed = mixed_ref[rows, cols] * near_scale + mixed * far_scale
            mixed = mixed / total
            level = top * SCALE + jnp.log(total)
            for i in range(chunk // slots):
                d = start // slots + i
                part = slice(i * slots, (i + 1) * slots)
                out_ref[d, h * slots : (h + 1) * slots, :] = mixed[part].astype(bf16)
                line = jnp.sum(
                    jnp.where(eye, level[part], 0.0), axis=0, keepdims=True
                )
                first = line.astype(bf16).astype(f32)
                second = (line - first).astype(bf16).astype(f32)
                third = line - first - second
                for p, piece in enumerate((first, second, third)):
                    stats[d] = jnp.where(row == base + p, stats[d] + piece, stats[d])
    for d in range(parts):
        out_ref[d, heads * slots : heads * slots + STAT, :] = stats[d].astype(bf16)


def attend_far(parts, queries, far, mixed, stat, slots, chunk):
    heads = queries.shape[1] // HD
    return pl.pallas_call(
        functools.partial(far_kernel, chunk=chunk),
        out_shape=pltpu.VMEM((parts, heads * slots + STAT, HD), bf16),
        in_specs=[VM] * 4,
        out_specs=VM,
        compiler_params=grant(20),
    )(*local(queries, far, mixed, stat))


def merge_kernel(got_ref, w_ref, out_ref):
    parts, rows, _ = got_ref.shape
    count = w_ref.shape[0] // HD
    slots = (rows - STAT) // count
    stat = got_ref[:, rows - STAT : rows, :].astype(f32)
    shares = []
    for base in range(0, 3 * ((count + 1) // 2), 3):
        level = stat[:, base] + stat[:, base + 1] + stat[:, base + 2]
        share = jnp.exp(level - jnp.max(level, axis=0, keepdims=True))
        share = share / jnp.sum(share, axis=0, keepdims=True)
        pad = jnp.zeros((HD - parts, HD), f32)
        shares.append(jnp.concatenate([share, pad], axis=0).T)
    heads = []
    for h in range(count):
        share = shares[h // 2][slots * (h % 2) : slots * (h % 2 + 1)]
        total = jnp.zeros((slots, HD), f32)
        for s in range(parts):
            block = got_ref[s, h * slots : (h + 1) * slots, :].astype(f32)
            total += block * share[:, s : s + 1]
        heads.append(total.astype(bf16))
    attended = jnp.concatenate(heads, axis=1)
    piece = out_ref.shape[2]
    for k in range(out_ref.shape[0]):
        out_ref[k] = jnp.dot(
            attended, w_ref[:, k * piece : (k + 1) * piece], preferred_element_type=f32
        ).astype(bf16)


def merge(got, w_out, groups):
    slots = (got.shape[1] - STAT) // (w_out.shape[0] // HD)
    return pl.pallas_call(
        merge_kernel,
        out_shape=pltpu.VMEM(
            (groups, slots, w_out.shape[1] // groups), bf16
        ),
        in_specs=[VM, VM],
        out_specs=VM,
        compiler_params=grant(8),
    )(*local(got, w_out))


def flat(ref):
    return jnp.concatenate([ref[i : i + 1, :] for i in range(ref.shape[0])], axis=1)


def norm_kernel(got_ref, hidden_ref, scale_ref, shift_ref, w_ref, out_ref):
    slots, width = hidden_ref.shape
    summed = hidden_ref[...].astype(f32)
    for k in range(got_ref.shape[0]):
        summed += got_ref[k].astype(f32)
    mean = jnp.sum(summed, axis=1, keepdims=True) * (1.0 / width)
    centred = summed - mean
    squares = jnp.sum(centred * centred, axis=1, keepdims=True)
    lifted = 1.0 + flat(scale_ref)
    tail = lax.broadcasted_iota(jnp.int32, (STAT, width), 0)
    tail = jnp.where(tail == 0, lifted, jnp.where(tail == 1, flat(shift_ref), 0.0))
    rows = jnp.concatenate([centred * lifted, tail], axis=0)
    mapped = lax.dot_general(
        rows,
        w_ref[...],
        (((1,), (1,)), ((), ())),
        precision=lax.Precision.HIGHEST,
        preferred_element_type=f32,
    )
    lane = lax.broadcasted_iota(jnp.int32, (slots, 64), 1)
    stat = jnp.where(lane == 0, mean, jnp.where(lane == 1, squares, 0.0))
    stat = jnp.concatenate([stat, jnp.zeros((STAT, 64), f32)], axis=0)
    block = jnp.concatenate([mapped, stat], axis=1)
    for k in range(out_ref.shape[0]):
        out_ref[k] = block


def norm(got, hidden, scale, shift, w_final):
    return pl.pallas_call(
        norm_kernel,
        out_shape=pltpu.VMEM(
            (got.shape[0], hidden.shape[0] + STAT, 2 * w_final.shape[1]), f32
        ),
        in_specs=[VM] * 5,
        out_specs=VM,
        compiler_params=grant(8),
    )(*local(got, hidden, scale, shift, w_final.T))


def finish_kernel(
    count_ref, step_ref, pos_ref, got_ref, latent_ref, old_ref, velocity_ref, next_ref
):
    groups, rows, _ = got_ref.shape
    slots = rows - STAT
    ch = latent_ref.shape[0]
    blocks = [got_ref[k] for k in range(groups)]
    means = [b[0:slots, ch : ch + 1] for b in blocks]
    mean = sum(means) * (1.0 / groups)
    width = D // groups
    var = sum(b[0:slots, ch + 1 : ch + 2] for b in blocks)
    var = (var + width * sum((m - mean) * (m - mean) for m in means)) * (1.0 / D)
    mapped = sum(
        b[0:slots, 0:ch] + (m - mean) * b[slots : slots + 1, 0:ch]
        for b, m in zip(blocks, means)
    )
    base = sum(b[slots + 1 : slots + 2, 0:ch] for b in blocks)
    fresh = mapped * lax.rsqrt(var + EPS) + base
    tokens = latent_ref.shape[1]
    pick = one_hot(pos_ref, count_ref, tokens, slots).astype(f32)
    keep = lax.dot_general(
        jnp.ones((8, slots), f32),
        pick,
        (((1,), (1,)), ((), ())),
        preferred_element_type=f32,
    )[0:1]
    chosen = lax.dot_general(
        fresh,
        pick,
        (((0,), (1,)), ((), ())),
        precision=lax.Precision.HIGHEST,
        preferred_element_type=f32,
    )
    velocity = jnp.where(keep < 0.5, old_ref[...], chosen)
    velocity_ref[...] = velocity
    next_ref[...] = latent_ref[...] + step_ref[0:1, :] * velocity


def finish(count, step_size, pos, got, latent, cached_velocity):
    velocity, following = pl.pallas_call(
        finish_kernel,
        out_shape=(
            jax.ShapeDtypeStruct(latent.shape[::-1], f32),
            jax.ShapeDtypeStruct(latent.shape[::-1], f32),
        ),
        in_specs=[VM] * 6,
        out_specs=(VM, VM),
        compiler_params=grant(8),
    )(count, *local(step_size), pos, *local(got, latent.T, cached_velocity.T))
    return velocity.T, following.T


def on_device(
    query,
    new_kv,
    cache_kv,
    text_kv,
    active,
    counts,
    hidden,
    w_out,
    mod_shift,
    mod_scale,
    w_final,
    latent,
    cached_velocity,
    step_size,
):
    groups = lax.axis_size("head")
    around = ("zh", "zq")
    parts = lax.axis_size(around)
    slots = query.shape[0]
    trade = [(0, 1), (1, 0)]

    count = counts.reshape(1, 1)
    pos = active.reshape(1, slots)
    filled, step_row = fill(count, step_size.reshape(1, 1), pos, new_kv, cache_kv)
    other = lax.ppermute(filled, "za", trade)
    gathered = lax.all_gather(query, "zq", axis=0, tiled=True)
    pair = spread(filled, other, lax.axis_size("y"))
    near = lax.all_to_all(pair, "y", 0, 0, tiled=True)
    gathered = lax.all_gather(gathered, "zh", axis=0, tiled=True)
    far = lax.ppermute(near, "core", trade)
    mixed, stat = attend_near(parts, around, gathered, near, text_kv, gathered.shape[0])
    partial = attend_far(
        parts, gathered, far, mixed, stat, slots, gathered.shape[0]
    )
    returned = lax.all_to_all(partial, around, 0, 0, tiled=True)
    terms = merge(returned, w_out, groups)
    terms = lax.all_to_all(terms, "head", 0, 0, tiled=True)
    stats = norm(
        terms, hidden, mod_scale.reshape(-1, 128), mod_shift.reshape(-1, 128), w_final
    )
    stats = lax.all_to_all(stats, "head", 0, 0, tiled=True)
    return finish(count, step_row, pos, stats, latent, cached_velocity)


def solution(mesh):
    in_specs = (
        P(SEQ, "head"),
        P(None, SEQ, "head"),
        P(None, SEQ, "head"),
        P(None, None, "head"),
        P(SEQ),
        P(SEQ),
        P(SEQ, "head"),
        P("head", None),
        P("head"),
        P("head"),
        P("head", None),
        P(SEQ, None),
        P(SEQ, None),
        P(),
    )
    out_specs = (P(SEQ, None), P(SEQ, None))
    split = jax.sharding.Mesh(
        mesh.devices.reshape(4, 2, 2, 4, 2, mesh.shape["head"]), SEQ + ("head",)
    )

    return jax.shard_map(
        on_device, mesh=split, in_specs=in_specs, out_specs=out_specs, check_vma=False
    )
```

```python
import functools

import jax
import jax.numpy as jnp
from jax import lax
from jax.experimental import pallas as pl
from jax.experimental.pallas import tpu as pltpu
from jax.sharding import PartitionSpec as P


D = 3072
HD = 128
EPS = 1e-06
LOG2E = 1.4426950408889634
SCALE = HD ** (-0.5)
SEQ = ("zh", "zq", "za", "y", "core")
STAT = 8


f32 = jnp.float32
bf16 = jnp.bfloat16
VM = pl.BlockSpec(memory_space=pltpu.VMEM)


def grant(mebibytes):
    return pltpu.CompilerParams(vmem_limit_bytes=mebibytes * 2**20)


def local(*arrays):
    return [pltpu.with_memory_space_constraint(x, pltpu.VMEM) for x in arrays]


def remote(*arrays):
    return [pltpu.with_memory_space_constraint(x, pltpu.HBM) for x in arrays]


def one_hot(pos_ref, count_ref, rows, cols):
    local = pos_ref[...] - lax.axis_index(SEQ) * rows
    slot = lax.broadcasted_iota(jnp.int32, (1, cols), 1)
    local = jnp.where(slot < count_ref[...], local, -1)
    return lax.broadcasted_iota(jnp.int32, (rows, cols), 0) == local


def fill_kernel(count_ref, step_ref, pos_ref, new_ref, cache_ref, out_ref, row_ref):
    rows, cols = cache_ref.shape[1], new_ref.shape[1]
    matched = one_hot(pos_ref, count_ref, rows, cols)
    pick = matched.astype(f32)
    keep = jnp.max(pick, axis=1, keepdims=True) < 0.5
    pick = pick.astype(bf16)
    for s in range(2):
        placed = jnp.dot(pick, new_ref[s], preferred_element_type=f32)
        merged = jnp.where(keep, cache_ref[s].astype(f32), placed).astype(bf16)
        out_ref[s] = merged
    row_ref[...] = jnp.broadcast_to(step_ref[...], row_ref.shape)


def fill(count, step_size, pos, new_kv, cache_kv):
    return pl.pallas_call(
        fill_kernel,
        out_shape=(
            pltpu.VMEM(cache_kv.shape, bf16),
            pltpu.VMEM((8, 128), f32),
        ),
        in_specs=[VM] * 5,
        out_specs=(VM, VM),
        compiler_params=grant(8),
    )(count, step_size, *remote(pos, new_kv, cache_kv))


def spread_kernel(own_ref, other_ref, out_ref, sems):
    copies = []
    for d in range(out_ref.shape[0]):
        for i, ref in enumerate((own_ref, other_ref)):
            copies.append(pltpu.make_async_copy(ref, out_ref.at[d, i], sems.at[d, i]))
    for copy in copies:
        copy.start()
    for copy in copies:
        copy.wait()


def spread(own, other, copies):
    return pl.pallas_call(
        spread_kernel,
        out_shape=pltpu.HBM((copies, 2) + own.shape, bf16),
        in_specs=[VM] * 2,
        out_specs=pl.BlockSpec(memory_space=pltpu.HBM),
        scratch_shapes=[pltpu.SemaphoreType.DMA((copies, 2))],
        compiler_params=grant(8),
    )(*local(own, other))


def attend_part(q, keys, values):
    scores = [
        lax.dot_general(q, k, (((1,), (1,)), ((), ())), preferred_element_type=f32)
        for k in keys
    ]
    top = functools.reduce(
        jnp.maximum, [jnp.max(s, axis=1, keepdims=True) for s in scores]
    )
    weights = [jnp.exp2((s - top) * (SCALE * LOG2E)) for s in scores]
    total = sum(jnp.sum(w, axis=1, keepdims=True) for w in weights)
    mixed = sum(
        jnp.dot(w.astype(bf16), v, preferred_element_type=f32)
        for w, v in zip(weights, values)
    )
    return top, total, mixed


def flat_keys(ref, side, cols):
    n = ref.shape[0] * ref.shape[1] * ref.shape[3]
    return ref[:, :, side, :, cols].reshape(n, HD)


def near_kernel(q_ref, a_ref, t_ref, mixed_ref, stat_ref, *, chunk, parts, around):
    share = t_ref.shape[1] // parts
    own_text = pl.ds(pl.multiple_of(lax.axis_index(around) * share, share), share)
    heads = q_ref.shape[1] // HD
    for start in range(0, q_ref.shape[0], chunk):
        rows = pl.ds(start, chunk)
        for h in range(heads):
            cols = slice(h * HD, (h + 1) * HD)
            top, total, mixed = attend_part(
                q_ref[rows, cols],
                [flat_keys(a_ref, 0, cols), t_ref[0, own_text, cols]],
                [flat_keys(a_ref, 1, cols), t_ref[1, own_text, cols]],
            )
            mixed_ref[rows, cols] = mixed
            stat_ref[0, rows, cols] = jnp.broadcast_to(top, (chunk, HD))
            stat_ref[1, rows, cols] = jnp.broadcast_to(total, (chunk, HD))


def attend_near(parts, around, queries, near, text_kv, chunk):
    return pl.pallas_call(
        functools.partial(near_kernel, chunk=chunk, parts=parts, around=around),
        out_shape=(
            pltpu.VMEM(queries.shape, f32),
            pltpu.VMEM((2,) + queries.shape, f32),
        ),
        in_specs=[VM] * 3,
        out_specs=(VM, VM),
        compiler_params=grant(20),
    )(*local(queries, near, text_kv))


def far_kernel(q_ref, b_ref, mixed_ref, stat_ref, out_ref, *, chunk):
    parts = out_ref.shape[0]
    slots = q_ref.shape[0] // parts
    heads = q_ref.shape[1] // HD
    lane = lax.broadcasted_iota(jnp.int32, (slots, HD), 1)
    slot = lax.broadcasted_iota(jnp.int32, (slots, HD), 0)
    row = lax.broadcasted_iota(jnp.int32, (STAT, HD), 0)
    stats = [jnp.zeros((STAT, HD), f32)] * parts
    for h in range(heads):
        cols = slice(h * HD, (h + 1) * HD)
        eye = lane == slot + slots * (h % 2)
        base = 3 * (h // 2)
        for start in range(0, q_ref.shape[0], chunk):
            rows = pl.ds(start, chunk)
            far_top, far_total, mixed = attend_part(
                q_ref[rows, cols],
                [flat_keys(b_ref, 0, cols)],
                [flat_keys(b_ref, 1, cols)],
            )
            near_top = stat_ref[0, rows, cols]
            near_total = stat_ref[1, rows, cols]
            far_top = jnp.broadcast_to(far_top, (chunk, HD))
            top = jnp.maximum(near_top, far_top)
            near_scale = jnp.exp2((near_top - top) * (SCALE * LOG2E))
            far_scale = jnp.exp2((far_top - top) * (SCALE * LOG2E))
            total = near_total * near_scale + far_total * far_scale
            mixed = mixed_ref[rows, cols] * near_scale + mixed * far_scale
            mixed = mixed / total
            level = top * SCALE + jnp.log(total)
            for i in range(chunk // slots):
                d = start // slots + i
                part = slice(i * slots, (i + 1) * slots)
                out_ref[d, h * slots : (h + 1) * slots, :] = mixed[part].astype(bf16)
                line = jnp.sum(
                    jnp.where(eye, level[part], 0.0), axis=0, keepdims=True
                )
                first = line.astype(bf16).astype(f32)
                second = (line - first).astype(bf16).astype(f32)
                third = line - first - second
                for p, piece in enumerate((first, second, third)):
                    stats[d] = jnp.where(row == base + p, stats[d] + piece, stats[d])
    for d in range(parts):
        out_ref[d, heads * slots : heads * slots + STAT, :] = stats[d].astype(bf16)


def attend_far(parts, queries, far, mixed, stat, slots, chunk):
    heads = queries.shape[1] // HD
    return pl.pallas_call(
        functools.partial(far_kernel, chunk=chunk),
        out_shape=pltpu.VMEM((parts, heads * slots + STAT, HD), bf16),
        in_specs=[VM] * 4,
        out_specs=VM,
        compiler_params=grant(20),
    )(*local(queries, far, mixed, stat))


def merge_kernel(got_ref, w_ref, out_ref):
    parts, rows, _ = got_ref.shape
    count = w_ref.shape[0] // HD
    slots = (rows - STAT) // count
    stat = got_ref[:, rows - STAT : rows, :].astype(f32)
    shares = []
    for base in range(0, 3 * ((count + 1) // 2), 3):
        level = stat[:, base] + stat[:, base + 1] + stat[:, base + 2]
        share = jnp.exp(level - jnp.max(level, axis=0, keepdims=True))
        share = share / jnp.sum(share, axis=0, keepdims=True)
        pad = jnp.zeros((HD - parts, HD), f32)
        shares.append(jnp.concatenate([share, pad], axis=0).T)
    heads = []
    for h in range(count):
        share = shares[h // 2][slots * (h % 2) : slots * (h % 2 + 1)]
        total = jnp.zeros((slots, HD), f32)
        for s in range(parts):
            block = got_ref[s, h * slots : (h + 1) * slots, :].astype(f32)
            total += block * share[:, s : s + 1]
        heads.append(total.astype(bf16))
    attended = jnp.concatenate(heads, axis=1)
    piece = out_ref.shape[2]
    for k in range(out_ref.shape[0]):
        out_ref[k] = jnp.dot(
            attended, w_ref[:, k * piece : (k + 1) * piece], preferred_element_type=f32
        ).astype(bf16)


def merge(got, w_out, groups):
    slots = (got.shape[1] - STAT) // (w_out.shape[0] // HD)
    return pl.pallas_call(
        merge_kernel,
        out_shape=pltpu.VMEM(
            (groups, slots, w_out.shape[1] // groups), bf16
        ),
        in_specs=[VM, VM],
        out_specs=VM,
        compiler_params=grant(8),
    )(*local(got, w_out))


def flat(ref):
    return jnp.concatenate([ref[i : i + 1, :] for i in range(ref.shape[0])], axis=1)


def norm_kernel(got_ref, hidden_ref, scale_ref, shift_ref, w_ref, out_ref):
    slots, width = hidden_ref.shape
    summed = hidden_ref[...].astype(f32)
    for k in range(got_ref.shape[0]):
        summed += got_ref[k].astype(f32)
    mean = jnp.sum(summed, axis=1, keepdims=True) * (1.0 / width)
    centred = summed - mean
    squares = jnp.sum(centred * centred, axis=1, keepdims=True)
    lifted = 1.0 + flat(scale_ref)
    tail = lax.broadcasted_iota(jnp.int32, (STAT, width), 0)
    tail = jnp.where(tail == 0, lifted, jnp.where(tail == 1, flat(shift_ref), 0.0))
    rows = jnp.concatenate([centred * lifted, tail], axis=0)
    mapped = lax.dot_general(
        rows,
        w_ref[...],
        (((1,), (1,)), ((), ())),
        precision=lax.Precision.HIGHEST,
        preferred_element_type=f32,
    )
    lane = lax.broadcasted_iota(jnp.int32, (slots, 64), 1)
    stat = jnp.where(lane == 0, mean, jnp.where(lane == 1, squares, 0.0))
    stat = jnp.concatenate([stat, jnp.zeros((STAT, 64), f32)], axis=0)
    block = jnp.concatenate([mapped, stat], axis=1)
    for k in range(out_ref.shape[0]):
        out_ref[k] = block


def norm(got, hidden, scale, shift, w_final):
    return pl.pallas_call(
        norm_kernel,
        out_shape=pltpu.VMEM(
            (got.shape[0], hidden.shape[0] + STAT, 2 * w_final.shape[1]), f32
        ),
        in_specs=[VM] * 5,
        out_specs=VM,
        compiler_params=grant(8),
    )(*local(got, hidden, scale, shift, w_final.T))


def finish_kernel(
    count_ref, step_ref, pos_ref, got_ref, latent_ref, old_ref, velocity_ref, next_ref
):
    groups, rows, _ = got_ref.shape
    slots = rows - STAT
    ch = latent_ref.shape[0]
    blocks = [got_ref[k] for k in range(groups)]
    means = [b[0:slots, ch : ch + 1] for b in blocks]
    mean = sum(means) * (1.0 / groups)
    width = D // groups
    var = sum(b[0:slots, ch + 1 : ch + 2] for b in blocks)
    var = (var + width * sum((m - mean) * (m - mean) for m in means)) * (1.0 / D)
    mapped = sum(
        b[0:slots, 0:ch] + (m - mean) * b[slots : slots + 1, 0:ch]
        for b, m in zip(blocks, means)
    )
    base = sum(b[slots + 1 : slots + 2, 0:ch] for b in blocks)
    fresh = mapped * lax.rsqrt(var + EPS) + base
    tokens = latent_ref.shape[1]
    pick = one_hot(pos_ref, count_ref, tokens, slots).astype(f32)
    keep = lax.dot_general(
        jnp.ones((8, slots), f32),
        pick,
        (((1,), (1,)), ((), ())),
        preferred_element_type=f32,
    )[0:1]
    chosen = lax.dot_general(
        fresh,
        pick,
        (((0,), (1,)), ((), ())),
        precision=lax.Precision.HIGHEST,
        preferred_element_type=f32,
    )
    velocity = jnp.where(keep < 0.5, old_ref[...], chosen)
    velocity_ref[...] = velocity
    next_ref[...] = latent_ref[...] + step_ref[0:1, :] * velocity


def finish(count, step_size, pos, got, latent, cached_velocity):
    velocity, following = pl.pallas_call(
        finish_kernel,
        out_shape=(
            jax.ShapeDtypeStruct(latent.shape[::-1], f32),
            jax.ShapeDtypeStruct(latent.shape[::-1], f32),
        ),
        in_specs=[VM] * 6,
        out_specs=(VM, VM),
        compiler_params=grant(8),
    )(count, *local(step_size), pos, *local(got, latent.T, cached_velocity.T))
    return velocity.T, following.T


def on_device(
    query,
    new_kv,
    cache_kv,
    text_kv,
    active,
    counts,
    hidden,
    w_out,
    mod_shift,
    mod_scale,
    w_final,
    latent,
    cached_velocity,
    step_size,
):
    groups = lax.axis_size("head")
    around = ("zh", "zq")
    parts = lax.axis_size(around)
    slots = query.shape[0]
    trade = [(0, 1), (1, 0)]

    count = counts.reshape(1, 1)
    pos = active.reshape(1, slots)
    filled, step_row = fill(count, step_size.reshape(1, 1), pos, new_kv, cache_kv)
    other = lax.ppermute(filled, "za", trade)
    gathered = lax.all_gather(query, "zq", axis=0, tiled=True)
    pair = spread(filled, other, lax.axis_size("y"))
    near = lax.all_to_all(pair, "y", 0, 0, tiled=True)
    gathered = lax.all_gather(gathered, "zh", axis=0, tiled=True)
    far = lax.ppermute(near, "core", trade)
    mixed, stat = attend_near(parts, around, gathered, near, text_kv, gathered.shape[0])
    partial = attend_far(
        parts, gathered, far, mixed, stat, slots, gathered.shape[0]
    )
    returned = lax.all_to_all(partial, around, 0, 0, tiled=True)
    terms = merge(returned, w_out, groups)
    terms = lax.all_to_all(terms, "head", 0, 0, tiled=True)
    stats = norm(
        terms, hidden, mod_scale.reshape(-1, 128), mod_shift.reshape(-1, 128), w_final
    )
    stats = lax.all_to_all(stats, "head", 0, 0, tiled=True)
    return finish(count, step_row, pos, stats, latent, cached_velocity)


def solution(mesh):
    in_specs = (
        P(SEQ, "head"),
        P(None, SEQ, "head"),
        P(None, SEQ, "head"),
        P(None, None, "head"),
        P(SEQ),
        P(SEQ),
        P(SEQ, "head"),
        P("head", None),
        P("head"),
        P("head"),
        P("head", None),
        P(SEQ, None),
        P(SEQ, None),
        P(),
    )
    out_specs = (P(SEQ, None), P(SEQ, None))
    split = jax.sharding.Mesh(
        mesh.devices.reshape(4, 2, 2, 4, 2, mesh.shape["head"]), SEQ + ("head",)
    )

    return jax.shard_map(
        on_device, mesh=split, in_specs=in_specs, out_specs=out_specs, check_vma=False
    )
```
